32 devices in a mesh: lat: 16 (over z, y, core), ma: 2 (over x).
Axes of the slice: x: 2, y: 2, z: 4, core: 2. Of those that a mesh axis runs over, the one named last changes fastest.
Arguments:
- spectral: bfloat16 [16, 2, 648, 768], P('ma'), may hold values from -0.25 to 0.25
- set_pair: int32 [16], P('ma'), may hold values from 0 to 639, as said below
- lat_sines: float32 [640], replicated, may hold values from 0.005 to 0.3
Outputs:
- grid: bfloat16 [1280, 16, 2, 768], P(('lat', 'ma'))
The draws below stay inside these ranges and needn't reach their ends.
Inputs may be any that keep to these rules, and one draw needn't show every extreme that they name: `set_pair`: the values are distinct; 0 and 639 both occur.
All inputs are finite; a program needn't handle non-finite values.
Results may differ from the reference program's by a relative error of at most 0.0058.
Values may be sent and summed in bfloat16 or wider, within the bound.
No kernel may reach another device: no remote copies, remote signals or barrier semaphores. Data moves between devices by JAX's collectives and lax.ppermute only.
A program may use at most 128 MiB of HBM per device.

```python
import jax
import jax.numpy as jnp
from jax import lax

M = 1280
NH = 648
COLS = 768
MSETS = 16
LATP = 640


def draw_set_pair(key, part):
    interior = jax.random.permutation(key, M // 2 - 2)[:MSETS - 2] + 1
    chosen = jnp.concatenate([jnp.array([0, M // 2 - 1], dtype=jnp.int32), interior.astype(jnp.int32)])
    placing = jax.random.permutation(jax.random.fold_in(key, 7), MSETS)
    return chosen[placing].astype(jnp.int32)


def steps_of(rng, extent, cuts, low, largest):
    factor_of, own = 1.0, jax.random.fold_in(rng, 6)
    for axis_at, shards_of in cuts:
        heights = jnp.exp(jax.random.uniform(jax.random.fold_in(own, axis_at), (shards_of,), jnp.float32, low / len(cuts), largest / len(cuts)))
        factor_of = factor_of * jnp.repeat(heights, extent[axis_at] // shards_of).reshape([-1 if axis == axis_at else 1 for axis in range(len(extent))])
    return factor_of


def normal_values(own_key, extent, scale, most, split=(), kind=jnp.bfloat16):
    drawn = scale * jax.random.normal(own_key, extent, jnp.float32)
    if split:
        drawn = drawn * steps_of(own_key, extent, split, -0.22, 0.18)
    return jnp.clip(drawn, -most, most).astype(kind)


def setup_inputs(seed: int = 0) -> dict:
    splits = jax.random.split(jax.random.key(seed), 4)
    spectral = normal_values(splits[0], (MSETS, 2, NH, COLS), NH ** -0.5, 0.25, ((0, 2),))
    set_pair = draw_set_pair(jax.random.fold_in(splits[3], 71), 0)
    lat_sines = jnp.clip(jax.random.uniform(splits[2], (LATP,), jnp.float32, 0.005, 0.3), 0.005, 0.3)
    return {"spectral": spectral, "set_pair": set_pair, "lat_sines": lat_sines}


def compose(earlier, later):
    return (later[0] * earlier[0] + later[1] * earlier[2], later[0] * earlier[1] + later[1] * earlier[3], later[2] * earlier[0] + later[3] * earlier[2], later[2] * earlier[1] + later[3] * earlier[3], later[0] * earlier[4] + later[1] * earlier[5] + later[4], later[2] * earlier[4] + later[3] * earlier[5] + later[5])

def legendre_runs(sines, pairs):
    positions = jnp.arange(M + 1, dtype=jnp.int32)[None, :]
    run_length = (M - pairs)[:, None]
    first_run = positions < run_length
    order_m = jnp.where(first_run, pairs[:, None], M - 1 - pairs[:, None]).astype(jnp.float32)
    offset_k = jnp.where(first_run, positions, positions - run_length).astype(jnp.float32)
    degree = order_m + offset_k
    recurring = offset_k > 0.5
    beyond_one = offset_k > 1.5
    prior_degree = degree - 1.0
    factor_a = jnp.sqrt(jnp.where(recurring, 4.0 * degree * degree - 1.0, 1.0) / jnp.where(recurring, degree * degree - order_m * order_m, 1.0))
    factor_b = jnp.sqrt(jnp.where(beyond_one, prior_degree * prior_degree - order_m * order_m, 0.0) / jnp.where(beyond_one, 4.0 * prior_degree * prior_degree - 1.0, 1.0))
    log_start = 0.5 * (lax.lgamma(order_m + 1.5) - lax.lgamma(order_m + 1.0) - lax.lgamma(jnp.ones_like(order_m) * 1.5)) + 0.5 * jnp.log(jnp.ones_like(order_m) * 0.5)
    log_cosine = jnp.log(1.0 - sines * sines)
    full_shape = (pairs.shape[0], sines.shape[0], M + 1)
    start_values = jnp.exp(log_start[:, None, :] + 0.5 * order_m[:, None, :] * log_cosine[None, :, None])
    recur_mask = recurring[:, None, :]
    upper_left = jnp.where(recur_mask, factor_a[:, None, :] * sines[None, :, None], 0.0).astype(jnp.float32)
    upper_right = jnp.broadcast_to(jnp.where(recur_mask, -(factor_a * factor_b)[:, None, :], 0.0), full_shape).astype(jnp.float32)
    lower_left = jnp.broadcast_to(jnp.where(recur_mask, 1.0, 0.0), full_shape).astype(jnp.float32)
    lower_right = jnp.zeros(full_shape, jnp.float32)
    offset_one = jnp.where(recur_mask, 0.0, start_values).astype(jnp.float32)
    offset_two = jnp.zeros(full_shape, jnp.float32)
    scanned = lax.associative_scan(compose, (upper_left, upper_right, lower_left, lower_right, offset_one, offset_two), axis=2)
    return scanned[4]

def parity_weights(values, pairs, parity):
    slot_index = jnp.arange(NH, dtype=jnp.int32)[None, :]
    run_length = (M - pairs)[:, None]
    first_count = (run_length + 1 - parity) // 2
    second_count = (pairs[:, None] + 2 - parity) // 2
    source = jnp.where(slot_index < first_count, 2 * slot_index + parity, run_length + 2 * (slot_index - first_count) + parity)
    source = jnp.clip(source, 0, M).astype(jnp.int32)
    picked = jnp.take_along_axis(values, source[:, None, :], axis=2)
    in_first = (slot_index < first_count)[:, None, :]
    in_second = ((slot_index >= first_count) & (slot_index < first_count + second_count))[:, None, :]
    return jnp.stack([jnp.where(in_first, picked, 0.0), jnp.where(in_second, picked, 0.0)], axis=2).astype(jnp.bfloat16)

def reference(spectral, set_pair, lat_sines):

    def one_set(operands):
        coeffs, pair_index = operands
        values = legendre_runs(lat_sines, pair_index[None])
        partials = []
        for parity in range(2):
            weights = lax.optimization_barrier(parity_weights(values, pair_index[None], parity)[0])
            summed = jnp.einsum('tje,ec->tjc', weights.astype(jnp.float32), coeffs[parity].astype(jnp.float32))
            partials.append(summed.astype(jnp.bfloat16))
        even_part, odd_part = lax.optimization_barrier((partials[0], partials[1]))
        even_sum = even_part.astype(jnp.float32)
        odd_sum = odd_part.astype(jnp.float32)
        return jnp.stack([(even_sum + odd_sum).astype(jnp.bfloat16), (even_sum - odd_sum).astype(jnp.bfloat16)])
    stacked = lax.map(one_set, (spectral, set_pair))
    return stacked.transpose(1, 2, 0, 3, 4).reshape(2 * LATP, MSETS, 2, COLS)
```

```python
import functools

import jax
import jax.numpy as jnp
from jax import lax
from jax.experimental import pallas as pl
from jax.experimental.pallas import tpu as pltpu
from jax.sharding import PartitionSpec as P

M = 1280
LANES = 128
F32 = jnp.float32
BF16 = jnp.bfloat16
CHUNKS = (2, 2, 2, 2)
VMEM = pl.BlockSpec(memory_space=pltpu.VMEM)
SMEM = pl.BlockSpec(memory_space=pltpu.SMEM)
ANY = pl.BlockSpec(memory_space=pl.ANY)
PARAMS = pltpu.CompilerParams(vmem_limit_bytes=48 << 20)


def start_sum(order):
    total = jnp.zeros((order.shape[0], LANES), F32)
    for block in range(M // LANES):
        k = lax.broadcasted_iota(jnp.int32, total.shape, 1) + (block * LANES + 1)
        total = total + jnp.where(k <= order, jnp.log(1.0 + 0.5 / k.astype(F32)), 0.0)
    return jnp.sum(total, axis=1, keepdims=True)


def coefficients(slot, parity, pair, first_count, count):
    first = slot < first_count
    order = jnp.where(first, pair, M - 1 - pair)
    offset = jnp.where(first, 2 * slot, 2 * (slot - first_count)) + parity
    valid = (offset >= 2) & (slot < count)
    degree = (order + offset).astype(F32)
    square = order.astype(F32) * order.astype(F32)

    def parts(k):
        return k * k - square, 4.0 * k * k - 1.0

    (u0, d0), (u1, d1), (u2, d2), (u3, d3) = (parts(degree - back) for back in range(4))
    u0 = jnp.where(valid, u0, 1.0)
    u1 = jnp.where(valid, u1, 1.0)
    a = jnp.sqrt((d1 / u1) * (d0 / u0))
    b = u1 / d1 + u2 / d2
    g = a * jnp.sqrt(jnp.maximum((u2 / d2) * (u3 / d3), 0.0))
    a, ab, g = (jnp.where(valid, value, 0.0) for value in (a, a * b, g))
    return a, ab, jnp.where(slot == 0, -1.0, g)


def legendre(pair_ref, sign_ref, x_ref, tab_ref, coef_ref, p_ref, pt_ref, sets, slots):
    rows = 2 * sets
    low = LANES // rows
    high = x_ref.shape[0]
    blocks = -(-slots // LANES)
    sub = lax.broadcasted_iota(jnp.int32, (rows, 1), 0)
    pair = jnp.zeros((rows, 1), jnp.int32)
    for s in range(sets):
        pair = jnp.where(sub % sets == s, pair_ref[s], pair)
    parity = sub // sets
    first_count = (M - pair + 1 - parity) // 2
    count = first_count + (pair + 2 - parity) // 2
    for block in range(blocks):
        slot = lax.broadcasted_iota(jnp.int32, (rows, LANES), 1) + block * LANES
        for c, table in enumerate(coefficients(slot, parity, pair, first_count, count)):
            tab_ref[pl.ds(c * rows, rows), pl.ds(block * LANES, LANES)] = table
    for c in range(3):
        for block in range(blocks):
            wide = jnp.concatenate(
                [
                    jnp.broadcast_to(tab_ref[pl.ds(c * rows + r, 1), pl.ds(block * LANES, LANES)], (low, LANES))
                    for r in range(rows)
                ],
                axis=0,
            )
            coef_ref[c, pl.ds(block * LANES, LANES), :] = wide.T
    def spread(column):
        return jnp.broadcast_to(
            jnp.concatenate([jnp.broadcast_to(column[r : r + 1], (low, LANES)) for r in range(rows)], axis=0).T[:1],
            (1, LANES),
        )

    order1 = pair
    order2 = M - 1 - pair
    logs1 = spread(start_sum(order1))
    logs2 = spread(start_sum(order2))
    lane_qs = lax.broadcasted_iota(jnp.int32, (1, LANES), 1) // low
    pair_lane = jnp.zeros((1, LANES), jnp.int32)
    for s in range(sets):
        pair_lane = jnp.where(lane_qs % sets == s, pair_ref[s], pair_lane)
    odd = lane_qs >= sets
    parity_lane = odd.astype(jnp.int32)
    first_lane = (M - pair_lane + 1 - parity_lane) // 2
    x = x_ref[...]
    x2 = x * x
    log_cos = jnp.log(1.0 - x2)
    sign = sign_ref[0]

    def seed(order, logs):
        m = order.astype(F32)
        value = jnp.exp(0.5 * (logs + jnp.log(jnp.full((1, LANES), 0.5, F32)) + m * log_cos))
        return jnp.where(odd, sign * jnp.sqrt(2.0 * m + 3.0) * x * value, value)

    seed1 = seed(pair_lane, logs1)
    seed2 = jnp.where(odd & (pair_lane < 1), 0.0, -seed(M - 1 - pair_lane, logs2))
    zero = jnp.zeros((high, LANES), F32)
    group = 32

    def steps(base, n, carry):
        last, before = carry
        for i in range(n):
            a, b, g = (coef_ref[c, pl.ds(base + i, 1), :] for c in range(3))
            tail = jnp.where(first_lane == base + i, seed2, g * before)
            now = (a * x2 - b) * last - tail
            p_ref[base + i, pl.ds(0, high), :] = now
            last, before = now, last
        return last, before

    carry = lax.fori_loop(
        0, slots // group, lambda t, c: steps(pl.multiple_of(t * group, group), group, c), (zero, seed1)
    )
    rest = slots % group
    if rest:
        steps(slots - rest, rest, carry)
    stride = p_ref.shape[1]


def weights_rows(p_ref, pt_ref, high, slots):
    blocks = -(-slots // LANES)
    for h in range(high):
        for block in range(blocks):
            tile = p_ref[pl.ds(block * LANES, LANES), h, :]
            pt_ref[pl.ds(h * LANES, LANES), pl.ds(block * LANES, LANES)] = tile.T


def project(pair_ref, pt_ref, spec, s, i, stage_ref, loc_ref, rem_ref, sets, slots, high):
    low = LANES // (2 * sets)
    band = high * low
    acc = None
    pair = pair_ref[s]
    for q in range(2):
        row = (q * sets + s) * low
        w = jnp.concatenate([pt_ref[pl.ds(h * LANES + row, low), pl.ds(0, slots)] for h in range(high)], axis=0)
        slot = lax.broadcasted_iota(jnp.int32, (band, slots), 1)
        first = slot < (M - pair + 1 - q) // 2
        lhs = jnp.concatenate([jnp.where(first, w, 0.0), jnp.where(first, 0.0, w)], axis=0).astype(BF16)
        part = jnp.dot(lhs, spec[q], preferred_element_type=F32)
        acc = part if acc is None else acc + part
    cols = acc.shape[1] // LANES
    for j in range(2):
        for c in range(cols):
            stage_ref[pl.ds(c * 2 + j, band, stride=2 * cols), :] = acc[j * band : (j + 1) * band, c * LANES : (c + 1) * LANES]
    cut = loc_ref.shape[1]
    loc_ref[i] = stage_ref[pl.ds(0, cut), :].astype(BF16)
    rem_ref[i] = stage_ref[pl.ds(cut, rem_ref.shape[1]), :].astype(BF16)


def first_kernel(pair_ref, sign_ref, x_ref, spec_ref, loc_ref, rem_ref, pt_ref, tab_ref, coef_ref, p_ref, buf_ref, stage_ref, sems, *, sets, slots, n):
    high = x_ref.shape[0]
    copies = [pltpu.make_async_copy(spec_ref.at[i], buf_ref.at[i], sems.at[i]) for i in range(n)]
    for copy in copies:
        copy.start()
    legendre(pair_ref, sign_ref, x_ref, tab_ref, coef_ref, p_ref, pt_ref, sets, slots)
    weights_rows(p_ref, pt_ref, high, slots)
    for i in range(n):
        copies[i].wait()
        project(pair_ref, pt_ref, buf_ref.at[i], i, i, stage_ref, loc_ref, rem_ref, sets, slots, high)


def next_kernel(pair_ref, pt_ref, spec_ref, loc_ref, rem_ref, buf_ref, stage_ref, sems, *, sets, slots, n, begin, high):
    copies = [pltpu.make_async_copy(spec_ref.at[begin + i], buf_ref.at[i], sems.at[i]) for i in range(n)]
    for copy in copies:
        copy.start()
    for i in range(n):
        copies[i].wait()
        project(pair_ref, pt_ref, buf_ref.at[i], begin + i, i, stage_ref, loc_ref, rem_ref, sets, slots, high)


def place_kernel(base_ref, *refs, plan, alias):
    parts = refs[: len(plan)]
    out_ref, sems = refs[-2], refs[-1]
    copies = []
    for part, (which, begin) in zip(parts, plan):
        for i in range(part.shape[0]):
            copies.append(
                pltpu.make_async_copy(part.at[i], out_ref.at[:, base_ref[which] + begin + i], sems.at[len(copies)])
            )
    for copy in copies:
        copy.start()
    for copy in copies:
        copy.wait()


def place(bases, parts, plan, shape, out=None):
    count = sum(part.shape[0] for part in parts)
    extra = () if out is None else (out,)
    return pl.pallas_call(
        functools.partial(place_kernel, plan=plan, alias=out is not None),
        in_specs=[SMEM] + [ANY] * (len(parts) + len(extra)),
        out_specs=ANY,
        out_shape=jax.ShapeDtypeStruct(shape, BF16),
        scratch_shapes=[pltpu.SemaphoreType.DMA((count,))],
        input_output_aliases={} if out is None else {1 + len(parts): 0},
        compiler_params=PARAMS,
    )(bases, *parts, *extra)


def local(spectral, set_pair, lat_sines):
    sets, _, slots, cols = spectral.shape
    half = lax.axis_size("lat") // 2
    peers = lax.axis_size("ma")
    lat_index = lax.axis_index("lat")
    ma = lax.axis_index("ma")
    band = lat_sines.shape[0] // half
    own = band // peers
    low = LANES // (2 * sets)
    high = band // low
    cb = cols // LANES
    sign = jnp.where(lat_index < half, 1.0, -1.0).astype(F32).reshape(1)
    rows = (lat_index % half) * band + (ma * own + jnp.arange(band, dtype=jnp.int32)) % band
    x = jnp.tile(lat_sines[rows].reshape(high, low), (1, 2 * sets))
    padded = -(-slots // LANES) * LANES
    pt_shape = jax.ShapeDtypeStruct((high * LANES, padded), F32)

    def shapes(n):
        return [
            jax.ShapeDtypeStruct((n, own * 2 * cb, LANES), BF16),
            jax.ShapeDtypeStruct((n, (band - own) * 2 * cb, LANES), BF16),
        ]

    def scratch(n):
        return [
            pltpu.VMEM((n, 2, slots, cols), BF16),
            pltpu.VMEM((band * 2 * cb, LANES), F32),
            pltpu.SemaphoreType.DMA((n,)),
        ]

    begins = [sum(CHUNKS[:k]) for k in range(len(CHUNKS))]
    locs, sent = [], []
    for k, n in enumerate(CHUNKS):
        if k == 0:
            loc, rem, pt = pl.pallas_call(
                functools.partial(first_kernel, sets=sets, slots=slots, n=n),
                in_specs=[SMEM, SMEM, VMEM, ANY],
                out_specs=[VMEM] * 3,
                out_shape=shapes(n) + [pt_shape],
                scratch_shapes=[
                    pltpu.VMEM((6 * sets, padded), F32),
                    pltpu.VMEM((3, padded, LANES), F32),
                    pltpu.VMEM((padded, -(-high // 8) * 8, LANES), F32),
                ]
                + scratch(n),
                compiler_params=PARAMS,
            )(set_pair, sign, x, spectral)
        else:
            loc, rem = pl.pallas_call(
                functools.partial(next_kernel, sets=sets, slots=slots, n=n, begin=begins[k], high=high),
                in_specs=[SMEM, VMEM, ANY],
                out_specs=[VMEM] * 2,
                out_shape=shapes(n),
                scratch_shapes=scratch(n),
                compiler_params=PARAMS,
            )(set_pair, pt, spectral)
        locs.append(loc.reshape(n, own, cb, 2, LANES))
        parts = rem.reshape(n, peers - 1, own * 2 * cb, LANES)
        got = []
        for d in range(1, peers):
            moved = lax.ppermute(parts[:, d - 1], "ma", [(i, (i + d) % peers) for i in range(peers)])
            got.append(moved.reshape(n, own, cb, 2, LANES))
        sent.append(got)
    bases = ((ma - jnp.arange(peers, dtype=jnp.int32)) % peers) * sets
    shape = (own, peers * sets, cb, 2, LANES)
    early = [(loc, (0, b)) for loc, b in zip(locs, begins)]
    late = []
    for k, got in enumerate(sent):
        (late if k == len(sent) - 1 else early).extend((g, (d + 1, begins[k])) for d, g in enumerate(got))
    out = place(bases, [p for p, _ in early], [w for _, w in early], shape)
    out = place(bases, [p for p, _ in late], [w for _, w in late], shape, out)
    return out.transpose(0, 1, 3, 2, 4).reshape(own, peers * sets, 2, cols)


def solution(mesh):
    placed = (P("ma", None, None, None), P("ma"), P())
    return jax.shard_map(
        local,
        mesh=mesh,
        in_specs=placed,
        out_specs=P(("lat", "ma"), None, None, None),
        check_vma=False,
    )
```

```python
import functools

import jax
import jax.numpy as jnp
from jax import lax
from jax.experimental import pallas as pl
from jax.experimental.pallas import tpu as pltpu
from jax.sharding import PartitionSpec as P


M = 1280
LANES = 128
F32 = jnp.float32
BF16 = jnp.bfloat16
CHUNKS = (1, 2, 2, 2, 1)
PIECES = 4
VMEM = pl.BlockSpec(memory_space=pltpu.VMEM)
SMEM = pl.BlockSpec(memory_space=pltpu.SMEM)
ANY = pl.BlockSpec(memory_space=pl.ANY)
HBM = pl.BlockSpec(memory_space=pltpu.HBM)
PARAMS = pltpu.CompilerParams(vmem_limit_bytes=40 << 20)


class Layout:
    def __init__(self, sets, slots, cols, band, own):
        self.sets, self.slots, self.cols, self.band, self.own = sets, slots, cols, band, own
        self.rows = 2 * sets
        self.low = LANES // self.rows
        self.blocks = -(-slots // LANES)
        self.padded = self.blocks * LANES
        self.cb = cols // LANES
        self.split = own % self.low == 0
        self.per_row = 2 * self.cb

    def high(self, count):
        return count // self.low

    def pitch(self, count):
        return -(-self.high(count) // 8) * 8


def coefficients(slot, parity, pair, first_count, count):
    first = slot < first_count
    order = jnp.where(first, pair, M - 1 - pair)
    offset = jnp.where(first, 2 * slot, 2 * (slot - first_count)) + parity
    valid = (offset >= 2) & (slot < count)
    degree = (order + offset).astype(F32)
    square = order.astype(F32) * order.astype(F32)

    def parts(k):
        return k * k - square, 4.0 * k * k - 1.0

    (u0, d0), (u1, d1), (u2, d2), (u3, d3) = (parts(degree - back) for back in range(4))
    u0 = jnp.where(valid, u0, 1.0)
    u1 = jnp.where(valid, u1, 1.0)
    a = jnp.sqrt((d1 / u1) * (d0 / u0))
    b = u1 / d1 + u2 / d2
    g = a * jnp.sqrt(jnp.maximum((u2 / d2) * (u3 / d3), 0.0))
    a, ab, g = (jnp.where(valid, value, 0.0) for value in (a, a * b, g))
    return a, ab, jnp.where(slot == 0, -1.0, g)


def table_block(lay, pair_ref, tab_ref, coef_ref, block):
    rows, sets, low = lay.rows, lay.sets, lay.low
    sub = lax.broadcasted_iota(jnp.int32, (rows, 1), 0)
    pair = jnp.zeros((rows, 1), jnp.int32)
    for s in range(sets):
        pair = jnp.where(sub % sets == s, pair_ref[s], pair)
    parity = sub // sets
    first_count = (M - pair + 1 - parity) // 2
    count = first_count + (pair + 2 - parity) // 2
    here = pl.ds(block * LANES, LANES)
    slot = lax.broadcasted_iota(jnp.int32, (rows, LANES), 1) + block * LANES
    for c, table in enumerate(coefficients(slot, parity, pair, first_count, count)):
        tab_ref[pl.ds(c * rows, rows), here] = table
    for c in range(3):
        wide = [jnp.broadcast_to(tab_ref[pl.ds(c * rows + r, 1), here], (low, LANES)) for r in range(rows)]
        coef_ref[c, here, :] = jnp.concatenate(wide, axis=0).T


def lane_values(lay, pair_ref):
    qs = lax.broadcasted_iota(jnp.int32, (1, LANES), 1) // lay.low
    pair = jnp.zeros((1, LANES), jnp.int32)
    for s in range(lay.sets):
        pair = jnp.where(qs % lay.sets == s, pair_ref[s], pair)
    return pair, qs // lay.sets


def seeds(lay, pair_ref, sign, x):
    sets = lay.sets
    sub = lax.broadcasted_iota(jnp.int32, (sets, 1), 0)
    column = jnp.zeros((sets, 1), jnp.int32)
    for s in range(sets):
        column = jnp.where(sub == s, pair_ref[s], column)
    lane_set = (lax.broadcasted_iota(jnp.int32, (sets, LANES), 1) // lay.low) % sets
    own_set = lane_set == lax.broadcasted_iota(jnp.int32, (sets, LANES), 0)
    pair, parity = lane_values(lay, pair_ref)
    odd = parity > 0
    log_cos = jnp.log(1.0 - x * x)

    def start(order_column, order):
        product = jnp.ones((sets, LANES), F32)
        for block in range(M // LANES):
            k = lax.broadcasted_iota(jnp.int32, (sets, LANES), 1) + (block * LANES + 1)
            product = product * jnp.where(k <= order_column, 1.0 + 0.5 / k.astype(F32), 1.0)
        logs = jnp.sum(jnp.log(product), axis=1, keepdims=True)
        logs = jnp.sum(jnp.where(own_set, logs, 0.0), axis=0, keepdims=True)
        m = order.astype(F32)
        value = jnp.exp(0.5 * (logs + jnp.log(jnp.full((1, LANES), 0.5, F32)) + m * log_cos))
        return jnp.where(odd, sign * jnp.sqrt(2.0 * m + 3.0) * x * value, value)

    first = start(column, pair)
    second = start(M - 1 - column, M - 1 - pair)
    return first, jnp.where(odd & (pair < 1), 0.0, -second)


def gather_rows(lay, sines_ref, begin, first_row, count):
    high = lay.high(count)
    lo = lax.broadcasted_iota(jnp.int32, (high, LANES), 1) % lay.low
    hi = lax.broadcasted_iota(jnp.int32, (high, LANES), 0)
    x = jnp.zeros((high, LANES), F32)
    for h in range(high):
        line = jnp.zeros((1, LANES), F32)
        for l in range(lay.low):
            row = first_row + (h * lay.low + l)
            row = jnp.where(row >= lay.band, row - lay.band, row)
            line = jnp.where(lo[:1] == l, sines_ref[begin + row], line)
        x = jnp.where(hi == h, line, x)
    return x


def legendre(lay, pair_ref, sign, x, coef_ref, p_ref, pt_ref, count, table):
    high, pitch = lay.high(count), lay.pitch(count)
    seed1, seed2 = seeds(lay, pair_ref, sign, x)
    pair, parity = lane_values(lay, pair_ref)
    switch = (M - pair + 1 - parity) // 2
    x2 = x * x
    last, before = jnp.zeros((high, LANES), F32), seed1

    def turn(block, h):
        n = min(LANES, lay.slots - block * LANES)
        tile = p_ref[pl.ds(block * LANES * pitch + h, n, stride=pitch), :]
        pt_ref[pl.ds(h * LANES, LANES), pl.ds(block * LANES, n)] = tile.T

    for block in range(lay.blocks):
        n = min(LANES, lay.slots - block * LANES)
        for i in range(n):
            slot = block * LANES + i
            if i == LANES // 8 and block + 1 < lay.blocks and table is not None:
                table(block + 1)
            if block and i >= LANES // 4 and (i - LANES // 4) % 8 == 0 and (i - LANES // 4) // 8 < high and n == LANES:
                turn(block - 1, (i - LANES // 4) // 8)
            a, b, g = (coef_ref[c, pl.ds(slot, 1), :] for c in range(3))
            tail = jnp.where(switch == slot, seed2, g * before) if slot >= 2 else g * before
            now = (a * x2 - b) * last - tail
            p_ref[pl.ds(slot * pitch, high), :] = now
            last, before = now, last
    whole = lay.slots // LANES
    for block in range(whole - 1, lay.blocks):
        for h in range(high):
            turn(block, h)


def project(lay, pair_ref, pt_ref, spec, s, stage_ref, count):
    acc = None
    pair = pair_ref[s]
    for q in range(2):
        row = (q * lay.sets + s) * lay.low
        w = jnp.concatenate(
            [pt_ref[pl.ds(h * LANES + row, lay.low), pl.ds(0, lay.slots)] for h in range(lay.high(count))], axis=0
        )
        first = lax.broadcasted_iota(jnp.int32, (count, lay.slots), 1) < (M - pair + 1 - q) // 2
        lhs = jnp.concatenate([jnp.where(first, w, 0.0), jnp.where(first, 0.0, w)], axis=0).astype(BF16)
        part = jnp.dot(lhs, spec[q], preferred_element_type=F32)
        acc = part if acc is None else acc + part
    for j in range(2):
        for c in range(lay.cb):
            stage_ref[pl.ds(c * 2 + j, count, stride=lay.per_row), :] = acc[
                j * count : (j + 1) * count, c * LANES : (c + 1) * LANES
            ]


def fetches(lay, spec_ref, buf_ref, sems, begin, n):
    step = lay.slots // PIECES // 16 * 16
    edges = [step * k for k in range(PIECES)] + [lay.slots]
    return [
        [
            pltpu.make_async_copy(
                spec_ref.at[begin + i, q, pl.ds(edges[k], edges[k + 1] - edges[k])],
                buf_ref.at[i, q, pl.ds(edges[k], edges[k + 1] - edges[k])],
                sems.at[i, q, k],
            )
            for q in range(2)
            for k in range(PIECES)
        ]
        for i in range(n)
    ]


def project_sets(lay, pair_ref, pt_ref, copies, buf_ref, stage_ref, out_ref, begin, n, count):
    for i in range(n):
        for copy in copies[i]:
            copy.wait()
        project(lay, pair_ref, pt_ref, buf_ref.at[i], begin + i, stage_ref, count)
        out_ref[i] = stage_ref[...].astype(BF16)


def position():
    half = lax.axis_size("lat") // 2
    lat = lax.axis_index("lat")
    return jnp.where(lat < half, 1.0, -1.0).astype(F32), lat % half, lax.axis_index("ma")


def head_kernel(
    pair_hbm, sines_hbm, spec_ref, out_ref, pt_ref, coef_ref, pair_ref, sines_ref, tab_ref, p_ref, buf_ref, stage_ref, small, sems,
    *, lay, n, count, offset,
):
    copies = fetches(lay, spec_ref, buf_ref, sems, 0, n)
    pair_copy = pltpu.make_async_copy(pair_hbm, pair_ref, small.at[0])
    sines_copy = pltpu.make_async_copy(sines_hbm, sines_ref, small.at[1])
    pair_copy.start()
    sines_copy.start()
    for group in copies:
        for copy in group:
            copy.start()
    sign, band, ma = position()
    pair_copy.wait()
    table_block(lay, pair_ref, tab_ref, coef_ref, 0)
    sines_copy.wait()
    x = gather_rows(lay, sines_ref, band * lay.band, ma * lay.own + offset, count)
    legendre(
        lay, pair_ref, sign, x, coef_ref, p_ref, pt_ref, count,
        lambda block: table_block(lay, pair_ref, tab_ref, coef_ref, block),
    )
    project_sets(lay, pair_ref, pt_ref, copies, buf_ref, stage_ref, out_ref, 0, n, count)


def next_kernel(pair_ref, pt_ref, spec_ref, out_ref, buf_ref, stage_ref, sems, *, lay, n, begin, count):
    copies = fetches(lay, spec_ref, buf_ref, sems, begin, n)
    for group in copies:
        for copy in group:
            copy.start()
    project_sets(lay, pair_ref, pt_ref, copies, buf_ref, stage_ref, out_ref, begin, n, count)


def own_kernel(
    pair_ref, sines_ref, coef_ref, spec_ref, out_ref, pt_ref, p_ref, buf_ref, stage_ref, sems, *, lay, n, count
):
    copies = fetches(lay, spec_ref, buf_ref, sems, 0, n)
    for group in copies:
        for copy in group:
            copy.start()
    sign, band, ma = position()
    x = gather_rows(lay, sines_ref, band * lay.band, ma * lay.own, count)
    legendre(lay, pair_ref, sign, x, coef_ref, p_ref, pt_ref, count, None)
    project_sets(lay, pair_ref, pt_ref, copies, buf_ref, stage_ref, out_ref, 0, n, count)


def place_kernel(base_ref, *refs, plan):
    parts = refs[: len(plan)]
    out_ref, sems = refs[-2], refs[-1]
    copies = []
    for part, (which, begin) in zip(parts, plan):
        for i in range(part.shape[0]):
            target = out_ref.at[:, base_ref[which] + begin + i]
            copies.append(pltpu.make_async_copy(part.at[i], target, sems.at[len(copies)]))
    for copy in copies:
        copy.start()
    for copy in copies:
        copy.wait()


def place(bases, parts, plan, shape, out=None):
    count = sum(part.shape[0] for part in parts)
    extra = () if out is None else (out,)
    return pl.pallas_call(
        functools.partial(place_kernel, plan=plan),
        in_specs=[SMEM] + [ANY] * (len(parts) + len(extra)),
        out_specs=ANY,
        out_shape=jax.ShapeDtypeStruct(shape, BF16),
        scratch_shapes=[pltpu.SemaphoreType.DMA((count,))],
        input_output_aliases={} if out is None else {1 + len(parts): 0},
        compiler_params=PARAMS,
    )(bases, *parts, *extra)


def transform(spectral, set_pair, lat_sines):
    sets, _, slots, cols = spectral.shape
    half = lax.axis_size("lat") // 2
    peers = lax.axis_size("ma")
    ma = lax.axis_index("ma")
    band = lat_sines.shape[0] // half
    own = band // peers
    lay = Layout(sets, slots, cols, band, own)
    offset = own if lay.split else 0
    count = band - offset
    cb = lay.cb

    def values(rows):
        return [
            jax.ShapeDtypeStruct((lay.high(rows) * LANES, lay.padded), F32),
            pltpu.VMEM((lay.padded * lay.pitch(rows), LANES), F32),
        ]

    def sums(n, rows):
        return [
            jax.ShapeDtypeStruct((n, rows * lay.per_row, LANES), BF16),
            pltpu.VMEM((n, 2, slots, cols), BF16),
            pltpu.VMEM((rows * lay.per_row, LANES), F32),
            pltpu.SemaphoreType.DMA((n, 2, PIECES)),
        ]

    begins = [sum(CHUNKS[:k]) for k in range(len(CHUNKS))]
    made = []
    for k, n in enumerate(CHUNKS):
        shape, *scratch = sums(n, count)
        if k == 0:
            pt_shape, p_scratch = values(count)
            coef_shape = jax.ShapeDtypeStruct((3, lay.padded, LANES), F32)
            made_now, pt, coef = pl.pallas_call(
                functools.partial(head_kernel, lay=lay, n=n, count=count, offset=offset),
                in_specs=[HBM, HBM, HBM],
                out_specs=[VMEM] * 3,
                out_shape=[shape, pt_shape, coef_shape],
                scratch_shapes=[
                    pltpu.SMEM(set_pair.shape, jnp.int32),
                    pltpu.SMEM(lat_sines.shape, F32),
                    pltpu.VMEM((3 * lay.rows, lay.padded), F32),
                    p_scratch,
                    *scratch[:2],
                    pltpu.SemaphoreType.DMA((2,)),
                    scratch[2],
                ],
                compiler_params=PARAMS,
            )(*(pltpu.with_memory_space_constraint(v, pltpu.HBM) for v in (set_pair, lat_sines)), spectral)
        else:
            made_now = pl.pallas_call(
                functools.partial(next_kernel, lay=lay, n=n, begin=begins[k], count=count),
                in_specs=[SMEM, VMEM, HBM],
                out_specs=VMEM,
                out_shape=shape,
                scratch_shapes=scratch,
                compiler_params=PARAMS,
            )(set_pair, pt, spectral)
        made.append(made_now.reshape(n, count // own, own * lay.per_row, LANES))

    first_peer = 0 if lay.split else 1
    early, late = [], []
    for k, (n, parts) in enumerate(zip(CHUNKS, made)):
        if not lay.split:
            early.append((parts[:, 0].reshape(n, own, cb, 2, LANES), (0, begins[k])))
        for d in range(1, peers):
            moved = lax.ppermute(parts[:, first_peer + d - 1], "ma", [(i, (i + d) % peers) for i in range(peers)])
            (late if k == len(CHUNKS) - 1 else early).append((moved.reshape(n, own, cb, 2, LANES), (d, begins[k])))
    if lay.split:
        shape, *scratch = sums(sets, own)
        pt_shape, p_scratch = values(own)
        mine = pl.pallas_call(
            functools.partial(own_kernel, lay=lay, n=sets, count=own),
            in_specs=[SMEM, SMEM, VMEM, HBM],
            out_specs=VMEM,
            out_shape=shape,
            scratch_shapes=[pltpu.VMEM(pt_shape.shape, F32), p_scratch, *scratch],
            compiler_params=PARAMS,
        )(set_pair, lat_sines, coef, spectral)
        early.append((mine.reshape(sets, own, cb, 2, LANES), (0, 0)))
    bases = ((ma - jnp.arange(peers, dtype=jnp.int32)) % peers) * sets
    shape = (own, peers * sets, cb, 2, LANES)
    out = place(bases, [p for p, _ in early], [w for _, w in early], shape)
    out = place(bases, [p for p, _ in late], [w for _, w in late], shape, out)
    return out.transpose(0, 1, 3, 2, 4).reshape(own, peers * sets, 2, cols)


def solution(mesh):
    placed = (P("ma", None, None, None), P("ma"), P())
    return jax.shard_map(
        transform,
        mesh=mesh,
        in_specs=placed,
        out_specs=P(("lat", "ma"), None, None, None),
        check_vma=False,
    )
```

```python
import functools

import jax
import jax.numpy as jnp
from jax import lax
from jax.experimental import pallas as pl
from jax.experimental.pallas import tpu as pltpu
from jax.sharding import PartitionSpec as P


M = 1280
LANES = 128
F32 = jnp.float32
BF16 = jnp.bfloat16
CHUNKS = (1, 2, 2, 2, 1)
AHEAD = 2
PIECES = 4
VMEM = pl.BlockSpec(memory_space=pltpu.VMEM)
SMEM = pl.BlockSpec(memory_space=pltpu.SMEM)
ANY = pl.BlockSpec(memory_space=pl.ANY)
HBM = pl.BlockSpec(memory_space=pltpu.HBM)
PARAMS = pltpu.CompilerParams(vmem_limit_bytes=24 << 20)


class Layout:
    def __init__(self, sets, slots, cols, band, own):
        self.sets, self.slots, self.cols, self.band, self.own = sets, slots, cols, band, own
        self.rows = 2 * sets
        self.low = LANES // self.rows
        self.blocks = -(-slots // LANES)
        self.padded = self.blocks * LANES
        self.cb = cols // LANES
        self.split = own % self.low == 0
        self.per_row = 2 * self.cb

    def high(self, count):
        return count // self.low

    def pitch(self, count):
        return -(-self.high(count) // 8) * 8


def coefficients(slot, parity, pair, first_count, count):
    first = slot < first_count
    order = jnp.where(first, pair, M - 1 - pair)
    offset = jnp.where(first, 2 * slot, 2 * (slot - first_count)) + parity
    valid = (offset >= 2) & (slot < count)
    degree = (order + offset).astype(F32)
    square = order.astype(F32) * order.astype(F32)

    def parts(k):
        return k * k - square, 4.0 * k * k - 1.0

    (u0, d0), (u1, d1), (u2, d2), (u3, d3) = (parts(degree - back) for back in range(4))
    u0 = jnp.where(valid, u0, 1.0)
    u1 = jnp.where(valid, u1, 1.0)
    a = jnp.sqrt((d1 / u1) * (d0 / u0))
    b = u1 / d1 + u2 / d2
    g = a * jnp.sqrt(jnp.maximum((u2 / d2) * (u3 / d3), 0.0))
    a, ab, g = (jnp.where(valid, value, 0.0) for value in (a, a * b, g))
    return a, ab, jnp.where(slot == 0, -1.0, g)


def table_block(lay, pair_ref, tab_ref, coef_ref, block):
    rows, sets, low = lay.rows, lay.sets, lay.low
    sub = lax.broadcasted_iota(jnp.int32, (rows, 1), 0)
    pair = jnp.zeros((rows, 1), jnp.int32)
    for s in range(sets):
        pair = jnp.where(sub % sets == s, pair_ref[s], pair)
    parity = sub // sets
    first_count = (M - pair + 1 - parity) // 2
    count = first_count + (pair + 2 - parity) // 2
    here = pl.ds(block * LANES, LANES)
    slot = lax.broadcasted_iota(jnp.int32, (rows, LANES), 1) + block * LANES
    for c, table in enumerate(coefficients(slot, parity, pair, first_count, count)):
        tab_ref[pl.ds(c * rows, rows), here] = table
    for c in range(3):
        wide = [jnp.broadcast_to(tab_ref[pl.ds(c * rows + r, 1), here], (low, LANES)) for r in range(rows)]
        coef_ref[c, here, :] = jnp.concatenate(wide, axis=0).T


def lane_values(lay, pair_ref):
    qs = lax.broadcasted_iota(jnp.int32, (1, LANES), 1) // lay.low
    pair = jnp.zeros((1, LANES), jnp.int32)
    for s in range(lay.sets):
        pair = jnp.where(qs % lay.sets == s, pair_ref[s], pair)
    return pair, qs // lay.sets


def seeds(lay, pair_ref, sign, x):
    sets = lay.sets
    sub = lax.broadcasted_iota(jnp.int32, (sets, 1), 0)
    column = jnp.zeros((sets, 1), jnp.int32)
    for s in range(sets):
        column = jnp.where(sub == s, pair_ref[s], column)
    lane_set = (lax.broadcasted_iota(jnp.int32, (sets, LANES), 1) // lay.low) % sets
    own_set = lane_set == lax.broadcasted_iota(jnp.int32, (sets, LANES), 0)
    pair, parity = lane_values(lay, pair_ref)
    odd = parity > 0
    log_cos = jnp.log(1.0 - x * x)

    def start(order_column, order):
        product = jnp.ones((sets, LANES), F32)
        for block in range(M // LANES):
            k = lax.broadcasted_iota(jnp.int32, (sets, LANES), 1) + (block * LANES + 1)
            product = product * jnp.where(k <= order_column, 1.0 + 0.5 / k.astype(F32), 1.0)
        logs = jnp.sum(jnp.log(product), axis=1, keepdims=True)
        logs = jnp.sum(jnp.where(own_set, logs, 0.0), axis=0, keepdims=True)
        m = order.astype(F32)
        value = jnp.exp(0.5 * (logs + jnp.log(jnp.full((1, LANES), 0.5, F32)) + m * log_cos))
        return jnp.where(odd, sign * jnp.sqrt(2.0 * m + 3.0) * x * value, value)

    first = start(column, pair)
    second = start(M - 1 - column, M - 1 - pair)
    return first, jnp.where(odd & (pair < 1), 0.0, -second)


def gather_rows(lay, sines_ref, begin, first_row, count):
    high = lay.high(count)
    lo = lax.broadcasted_iota(jnp.int32, (high, LANES), 1) % lay.low
    hi = lax.broadcasted_iota(jnp.int32, (high, LANES), 0)
    x = jnp.zeros((high, LANES), F32)
    for h in range(high):
        line = jnp.zeros((1, LANES), F32)
        for l in range(lay.low):
            row = first_row + (h * lay.low + l)
            row = jnp.where(row >= lay.band, row - lay.band, row)
            line = jnp.where(lo[:1] == l, sines_ref[begin + row], line)
        x = jnp.where(hi == h, line, x)
    return x


def legendre(lay, pair_ref, sign, x, coef_ref, p_ref, pt_ref, count, table):
    high, pitch = lay.high(count), lay.pitch(count)
    seed1, seed2 = seeds(lay, pair_ref, sign, x)
    pair, parity = lane_values(lay, pair_ref)
    switch = (M - pair + 1 - parity) // 2
    x2 = x * x
    last, before = jnp.zeros((high, LANES), F32), seed1

    def turn(block, h):
        n = min(LANES, lay.slots - block * LANES)
        tile = p_ref[pl.ds(block * LANES * pitch + h, n, stride=pitch), :]
        pt_ref[pl.ds(h * LANES, LANES), pl.ds(block * LANES, n)] = tile.T

    for block in range(lay.blocks):
        n = min(LANES, lay.slots - block * LANES)
        for i in range(n):
            slot = block * LANES + i
            if i == LANES // 8 and block + 1 < lay.blocks and table is not None:
                table(block + 1)
            if block and i >= LANES // 4 and (i - LANES // 4) % 8 == 0 and (i - LANES // 4) // 8 < high and n == LANES:
                turn(block - 1, (i - LANES // 4) // 8)
            a, b, g = (coef_ref[c, pl.ds(slot, 1), :] for c in range(3))
            tail = jnp.where(switch == slot, seed2, g * before) if slot >= 2 else g * before
            now = (a * x2 - b) * last - tail
            p_ref[pl.ds(slot * pitch, high), :] = now
            last, before = now, last
    whole = lay.slots // LANES
    for block in range(whole - 1, lay.blocks):
        for h in range(high):
            turn(block, h)


def project(lay, pair_ref, groups, spec, s):
    acc = None
    pair = pair_ref[s]
    here = pl.ds(0, lay.slots)
    for q in range(2):
        base = (q * lay.sets + s) * lay.low
        parts = []
        for pt_ref, count, _, _ in groups:
            w = jnp.concatenate(
                [pt_ref[pl.ds(h * LANES + base, lay.low), here] for h in range(lay.high(count))], axis=0
            )
            first = lax.broadcasted_iota(jnp.int32, (count, lay.slots), 1) < (M - pair + 1 - q) // 2
            parts += [jnp.where(first, w, 0.0), jnp.where(first, 0.0, w)]
        part = jnp.dot(jnp.concatenate(parts, axis=0).astype(BF16), spec[q], preferred_element_type=F32)
        acc = part if acc is None else acc + part
    row = 0
    for _, count, stage_ref, out_ref in groups:
        for j in range(2):
            for c in range(lay.cb):
                stage_ref[pl.ds(c * 2 + j, count, stride=lay.per_row), :] = acc[
                    row : row + count, c * LANES : (c + 1) * LANES
                ]
            row += count
        out_ref[...] = stage_ref[...].astype(BF16)


def fetches(lay, spec_ref, buf_ref, sems, begin, n):
    step = lay.slots // PIECES // 16 * 16
    edges = [step * k for k in range(PIECES)] + [lay.slots]
    return [
        [
            pltpu.make_async_copy(
                spec_ref.at[begin + i, q, pl.ds(edges[k], edges[k + 1] - edges[k])],
                buf_ref.at[i, q, pl.ds(edges[k], edges[k + 1] - edges[k])],
                sems.at[i, q, k],
            )
            for q in range(2)
            for k in range(PIECES)
        ]
        for i in range(n)
    ]


def begin_all(copies):
    for group in copies:
        for copy in group:
            copy.start()


def wait_all(copies):
    for copy in copies:
        copy.wait()


def position():
    half = lax.axis_size("lat") // 2
    lat = lax.axis_index("lat")
    return jnp.where(lat < half, 1.0, -1.0).astype(F32), lat % half, lax.axis_index("ma")


def head_kernel(
    pair_hbm, sines_hbm, spec_ref, out_ref, pt_ref, coef_ref, buf_ref, pair_ref, sines_ref, tab_ref, p_ref, stage_ref, small, sems,
    *, lay, n, count, offset,
):
    kept = buf_ref.shape[0]
    copies = fetches(lay, spec_ref, buf_ref, sems, 0, kept)
    pair_copy = pltpu.make_async_copy(pair_hbm, pair_ref, small.at[0])
    sines_copy = pltpu.make_async_copy(sines_hbm, sines_ref, small.at[1])
    pair_copy.start()
    sines_copy.start()
    begin_all(copies)
    sign, band, ma = position()
    pair_copy.wait()
    table_block(lay, pair_ref, tab_ref, coef_ref, 0)
    sines_copy.wait()
    x = gather_rows(lay, sines_ref, band * lay.band, ma * lay.own + offset, count)
    legendre(
        lay, pair_ref, sign, x, coef_ref, p_ref, pt_ref, count,
        lambda block: table_block(lay, pair_ref, tab_ref, coef_ref, block),
    )
    for i in range(kept):
        wait_all(copies[i])
        if i < n:
            project(lay, pair_ref, [(pt_ref, count, stage_ref, out_ref.at[i])], buf_ref.at[i], i)


def kept_kernel(pair_ref, pt_ref, buf_ref, out_ref, stage_ref, *, lay, begin, count):
    for i in range(out_ref.shape[0]):
        project(lay, pair_ref, [(pt_ref, count, stage_ref, out_ref.at[i])], buf_ref.at[begin + i], begin + i)


def own_kernel(pair_ref, pt_ref, spec_ref, out_ref, buf_ref, stage_ref, sems, *, lay):
    n = out_ref.shape[0]
    copies = fetches(lay, spec_ref, buf_ref, sems, 0, n)
    begin_all(copies)
    for i in range(n):
        wait_all(copies[i])
        project(lay, pair_ref, [(pt_ref, lay.own, stage_ref, out_ref.at[i])], buf_ref.at[i], i)


def late_kernel(*refs, lay, n, begin, count, make):
    refs = list(refs)
    pair_ref = refs.pop(0)
    if make:
        sines_ref, coef_ref = refs.pop(0), refs.pop(0)
    pt_ref = refs.pop(0)
    if lay.split and not make:
        own_pt_ref = refs.pop(0)
    spec_ref, out_ref = refs.pop(0), refs.pop(0)
    if lay.split:
        own_ref = refs.pop(0)
    if make:
        own_pt_ref = refs.pop(0)
    buf_ref, stage_ref, sems = refs.pop(0), refs.pop(0), refs.pop(0)
    copies = fetches(lay, spec_ref, buf_ref, sems, begin, n)
    begin_all(copies)
    if lay.split:
        own_stage_ref = refs.pop(0)
    if make:
        p_ref = refs.pop(0)
        sign, band, ma = position()
        x = gather_rows(lay, sines_ref, band * lay.band, ma * lay.own, lay.own)
        legendre(lay, pair_ref, sign, x, coef_ref, p_ref, own_pt_ref, lay.own, None)
    for i in range(n):
        wait_all(copies[i])
        groups = [(pt_ref, count, stage_ref, out_ref.at[i])]
        if lay.split:
            groups.append((own_pt_ref, lay.own, own_stage_ref, own_ref.at[i]))
        project(lay, pair_ref, groups, buf_ref.at[i], begin + i)


def place_kernel(base_ref, *refs, plan):
    parts = refs[: len(plan)]
    out_ref, sems = refs[-2], refs[-1]
    copies = []
    for part, (which, begin) in zip(parts, plan):
        for i in range(part.shape[0]):
            target = out_ref.at[:, base_ref[which] + begin + i]
            copies.append(pltpu.make_async_copy(part.at[i], target, sems.at[len(copies)]))
    for copy in copies:
        copy.start()
    for copy in copies:
        copy.wait()


def place(bases, parts, plan, shape, out=None):
    count = sum(part.shape[0] for part in parts)
    extra = () if out is None else (out,)
    return pl.pallas_call(
        functools.partial(place_kernel, plan=plan),
        in_specs=[SMEM] + [ANY] * (len(parts) + len(extra)),
        out_specs=ANY,
        out_shape=jax.ShapeDtypeStruct(shape, BF16),
        scratch_shapes=[pltpu.SemaphoreType.DMA((count,))],
        input_output_aliases={} if out is None else {1 + len(parts): 0},
        compiler_params=PARAMS,
    )(bases, *parts, *extra)


def transform(spectral, set_pair, lat_sines):
    sets, _, slots, cols = spectral.shape
    half = lax.axis_size("lat") // 2
    peers = lax.axis_size("ma")
    ma = lax.axis_index("ma")
    band = lat_sines.shape[0] // half
    own = band // peers
    lay = Layout(sets, slots, cols, band, own)
    offset = own if lay.split else 0
    count = band - offset
    cb = lay.cb

    split = lay.split
    pt_shape = jax.ShapeDtypeStruct((lay.high(count) * LANES, lay.padded), F32)
    own_pt_shape = jax.ShapeDtypeStruct((lay.high(own) * LANES, lay.padded), F32)
    coef_shape = jax.ShapeDtypeStruct((3, lay.padded, LANES), F32)

    def p_scratch(rows):
        return pltpu.VMEM((lay.padded * lay.pitch(rows), LANES), F32)

    def out_shape(n, rows):
        return jax.ShapeDtypeStruct((n, rows * lay.per_row, LANES), BF16)

    def stage(rows):
        return pltpu.VMEM((rows * lay.per_row, LANES), F32)

    def keep(value):
        return pltpu.with_memory_space_constraint(value, pltpu.HBM)

    def call(kernel, in_specs, shapes, scratch, args):
        return pl.pallas_call(
            kernel,
            in_specs=in_specs,
            out_specs=[VMEM] * len(shapes),
            out_shape=shapes,
            scratch_shapes=scratch,
            compiler_params=PARAMS,
        )(*args)

    begins = [sum(CHUNKS[:k]) for k in range(len(CHUNKS))]
    kept = sum(CHUNKS[:AHEAD])
    made, mine = [], []
    for k, n in enumerate(CHUNKS):
        if k == 0:
            sent, pt, coef, buf = call(
                functools.partial(head_kernel, lay=lay, n=n, count=count, offset=offset),
                [HBM] * 3,
                [out_shape(n, count), pt_shape, coef_shape, jax.ShapeDtypeStruct((kept, 2, slots, cols), BF16)],
                [
                    pltpu.SMEM(set_pair.shape, jnp.int32),
                    pltpu.SMEM(lat_sines.shape, F32),
                    pltpu.VMEM((3 * lay.rows, lay.padded), F32),
                    p_scratch(count),
                    stage(count),
                    pltpu.SemaphoreType.DMA((2,)),
                    pltpu.SemaphoreType.DMA((kept, 2, PIECES)),
                ],
                [keep(set_pair), keep(lat_sines), keep(spectral)],
            )
        elif k < AHEAD:
            (sent,) = call(
                functools.partial(kept_kernel, lay=lay, begin=begins[k], count=count),
                [SMEM, VMEM, VMEM],
                [out_shape(n, count)],
                [stage(count)],
                [set_pair, pt, buf],
            )
        else:
            make = split and k == AHEAD
            operands = [(SMEM, set_pair)]
            if make:
                operands += [(SMEM, lat_sines), (VMEM, coef)]
            operands.append((VMEM, pt))
            if split and not make:
                operands.append((VMEM, own_pt))
            operands.append((HBM, keep(spectral)))
            shapes = [out_shape(n, count)]
            scratch = [
                pltpu.VMEM((n, 2, slots, cols), BF16),
                stage(count),
                pltpu.SemaphoreType.DMA((n, 2, PIECES)),
            ]
            if split:
                shapes.append(out_shape(n, own))
                scratch.append(stage(own))
            if make:
                shapes.append(own_pt_shape)
                scratch.append(p_scratch(own))
            made_now = call(
                functools.partial(late_kernel, lay=lay, n=n, begin=begins[k], count=count, make=make),
                [spec for spec, _ in operands],
                shapes,
                scratch,
                [value for _, value in operands],
            )
            sent = made_now[0]
            if split:
                mine.append((made_now[1], begins[k]))
            if make:
                own_pt = made_now[2]
        made.append(sent.reshape(n, count // own, own * lay.per_row, LANES))

    first_peer = 0 if split else 1
    early, late = [], []
    for k, (n, parts) in enumerate(zip(CHUNKS, made)):
        if not split:
            mine.append((parts[:, 0], begins[k]))
        for d in range(1, peers):
            moved = lax.ppermute(parts[:, first_peer + d - 1], "ma", [(i, (i + d) % peers) for i in range(peers)])
            (late if k == len(CHUNKS) - 1 else early).append((moved.reshape(n, own, cb, 2, LANES), (d, begins[k])))
    if split:
        (first_own,) = call(
            functools.partial(own_kernel, lay=lay),
            [SMEM, VMEM, HBM],
            [out_shape(kept, own)],
            [
                pltpu.VMEM((kept, 2, slots, cols), BF16),
                stage(own),
                pltpu.SemaphoreType.DMA((kept, 2, PIECES)),
            ],
            [set_pair, own_pt, keep(spectral)],
        )
        mine.append((first_own, 0))
    early = [(part.reshape(part.shape[0], own, cb, 2, LANES), (0, begin)) for part, begin in mine] + early
    bases = ((ma - jnp.arange(peers, dtype=jnp.int32)) % peers) * sets
    shape = (own, peers * sets, cb, 2, LANES)
    out = place(bases, [p for p, _ in early], [w for _, w in early], shape)
    out = place(bases, [p for p, _ in late], [w for _, w in late], shape, out)
    return out.transpose(0, 1, 3, 2, 4).reshape(own, peers * sets, 2, cols)


def solution(mesh):
    placed = (P("ma", None, None, None), P("ma"), P())
    return jax.shard_map(
        transform,
        mesh=mesh,
        in_specs=placed,
        out_specs=P(("lat", "ma"), None, None, None),
        check_vma=False,
    )
```

```python
import functools

import jax
import jax.numpy as jnp
from jax import lax
from jax.experimental import pallas as pl
from jax.experimental.pallas import tpu as pltpu
from jax.sharding import PartitionSpec as P


M = 1280
LANES = 128
F32 = jnp.float32
BF16 = jnp.bfloat16
CHUNKS = (1, 2, 2, 2, 1)
AHEAD = 2
PIECES = 4
VMEM = pl.BlockSpec(memory_space=pltpu.VMEM)
SMEM = pl.BlockSpec(memory_space=pltpu.SMEM)
ANY = pl.BlockSpec(memory_space=pl.ANY)
HBM = pl.BlockSpec(memory_space=pltpu.HBM)
PARAMS = pltpu.CompilerParams(vmem_limit_bytes=16 << 20)


class Layout:
    def __init__(self, sets, slots, cols, band, own):
        self.sets, self.slots, self.cols, self.band, self.own = sets, slots, cols, band, own
        self.rows = 2 * sets
        self.low = LANES // self.rows
        self.blocks = -(-slots // LANES)
        self.padded = self.blocks * LANES
        self.cb = cols // LANES
        self.split = own % self.low == 0
        self.per_row = 2 * self.cb

    def high(self, count):
        return count // self.low

    def pitch(self, count):
        return -(-self.high(count) // 8) * 8


def coefficients(slot, parity, pair, first_count, count):
    first = slot < first_count
    order = jnp.where(first, pair, M - 1 - pair)
    offset = jnp.where(first, 2 * slot, 2 * (slot - first_count)) + parity
    valid = (offset >= 2) & (slot < count)
    degree = (order + offset).astype(F32)
    square = order.astype(F32) * order.astype(F32)

    def parts(k):
        return k * k - square, 4.0 * k * k - 1.0

    (u0, d0), (u1, d1), (u2, d2), (u3, d3) = (parts(degree - back) for back in range(4))
    u0 = jnp.where(valid, u0, 1.0)
    u1 = jnp.where(valid, u1, 1.0)
    a = jnp.sqrt((d1 / u1) * (d0 / u0))
    b = u1 / d1 + u2 / d2
    g = a * jnp.sqrt(jnp.maximum((u2 / d2) * (u3 / d3), 0.0))
    a, ab, g = (jnp.where(valid, value, 0.0) for value in (a, a * b, g))
    return a, ab, jnp.where(slot == 0, -1.0, g)


def table_block(lay, pair_ref, tab_ref, coef_ref, block):
    rows, sets, low = lay.rows, lay.sets, lay.low
    sub = lax.broadcasted_iota(jnp.int32, (rows, 1), 0)
    pair = jnp.zeros((rows, 1), jnp.int32)
    for s in range(sets):
        pair = jnp.where(sub % sets == s, pair_ref[s], pair)
    parity = sub // sets
    first_count = (M - pair + 1 - parity) // 2
    count = first_count + (pair + 2 - parity) // 2
    here = pl.ds(block * LANES, LANES)
    slot = lax.broadcasted_iota(jnp.int32, (rows, LANES), 1) + block * LANES
    for c, table in enumerate(coefficients(slot, parity, pair, first_count, count)):
        tab_ref[pl.ds(c * rows, rows), here] = table
    for c in range(3):
        wide = [jnp.broadcast_to(tab_ref[pl.ds(c * rows + r, 1), here], (low, LANES)) for r in range(rows)]
        coef_ref[c, here, :] = jnp.concatenate(wide, axis=0).T


def lane_values(lay, pair_ref):
    qs = lax.broadcasted_iota(jnp.int32, (1, LANES), 1) // lay.low
    pair = jnp.zeros((1, LANES), jnp.int32)
    for s in range(lay.sets):
        pair = jnp.where(qs % lay.sets == s, pair_ref[s], pair)
    return pair, qs // lay.sets


def seeds(lay, pair_ref, sign, x):
    sets = lay.sets
    sub = lax.broadcasted_iota(jnp.int32, (sets, 1), 0)
    column = jnp.zeros((sets, 1), jnp.int32)
    for s in range(sets):
        column = jnp.where(sub == s, pair_ref[s], column)
    lane_set = (lax.broadcasted_iota(jnp.int32, (sets, LANES), 1) // lay.low) % sets
    own_set = lane_set == lax.broadcasted_iota(jnp.int32, (sets, LANES), 0)
    pair, parity = lane_values(lay, pair_ref)
    odd = parity > 0
    log_cos = jnp.log(1.0 - x * x)

    def start(order_column, order):
        product = jnp.ones((sets, LANES), F32)
        for block in range(M // LANES):
            k = lax.broadcasted_iota(jnp.int32, (sets, LANES), 1) + (block * LANES + 1)
            product = product * jnp.where(k <= order_column, 1.0 + 0.5 / k.astype(F32), 1.0)
        logs = jnp.sum(jnp.log(product), axis=1, keepdims=True)
        logs = jnp.sum(jnp.where(own_set, logs, 0.0), axis=0, keepdims=True)
        m = order.astype(F32)
        value = jnp.exp(0.5 * (logs + jnp.log(jnp.full((1, LANES), 0.5, F32)) + m * log_cos))
        return jnp.where(odd, sign * jnp.sqrt(2.0 * m + 3.0) * x * value, value)

    first = start(column, pair)
    second = start(M - 1 - column, M - 1 - pair)
    return first, jnp.where(odd & (pair < 1), 0.0, -second)


def gather_rows(lay, sines_ref, begin, first_row, count):
    high = lay.high(count)
    lo = lax.broadcasted_iota(jnp.int32, (high, LANES), 1) % lay.low
    hi = lax.broadcasted_iota(jnp.int32, (high, LANES), 0)
    x = jnp.zeros((high, LANES), F32)
    for h in range(high):
        line = jnp.zeros((1, LANES), F32)
        for l in range(lay.low):
            row = first_row + (h * lay.low + l)
            row = jnp.where(row >= lay.band, row - lay.band, row)
            line = jnp.where(lo[:1] == l, sines_ref[begin + row], line)
        x = jnp.where(hi == h, line, x)
    return x


def legendre(lay, pair_ref, sign, x, coef_ref, p_ref, pt_ref, count, table):
    high, pitch = lay.high(count), lay.pitch(count)
    seed1, seed2 = seeds(lay, pair_ref, sign, x)
    pair, parity = lane_values(lay, pair_ref)
    switch = (M - pair + 1 - parity) // 2
    x2 = x * x
    last, before = jnp.zeros((high, LANES), F32), seed1

    def turn(block, h):
        n = min(LANES, lay.slots - block * LANES)
        tile = p_ref[pl.ds(block * LANES * pitch + h, n, stride=pitch), :]
        pt_ref[pl.ds(h * LANES, LANES), pl.ds(block * LANES, n)] = tile.T

    for block in range(lay.blocks):
        n = min(LANES, lay.slots - block * LANES)
        for i in range(n):
            slot = block * LANES + i
            if i == LANES // 8 and block + 1 < lay.blocks and table is not None:
                table(block + 1)
            if block and i >= LANES // 4 and (i - LANES // 4) % 8 == 0 and (i - LANES // 4) // 8 < high and n == LANES:
                turn(block - 1, (i - LANES // 4) // 8)
            a, b, g = (coef_ref[c, pl.ds(slot, 1), :] for c in range(3))
            tail = jnp.where(switch == slot, seed2, g * before) if slot >= 2 else g * before
            now = (a * x2 - b) * last - tail
            p_ref[pl.ds(slot * pitch, high), :] = now
            last, before = now, last
    whole = lay.slots // LANES
    for block in range(whole - 1, lay.blocks):
        for h in range(high):
            turn(block, h)


def project(lay, pair_ref, groups, spec, s):
    acc = None
    pair = pair_ref[s]
    here = pl.ds(0, lay.slots)
    for q in range(2):
        base = (q * lay.sets + s) * lay.low
        parts = []
        for pt_ref, count, _, _ in groups:
            w = jnp.concatenate(
                [pt_ref[pl.ds(h * LANES + base, lay.low), here] for h in range(lay.high(count))], axis=0
            )
            first = lax.broadcasted_iota(jnp.int32, (count, lay.slots), 1) < (M - pair + 1 - q) // 2
            parts += [jnp.where(first, w, 0.0), jnp.where(first, 0.0, w)]
        part = jnp.dot(jnp.concatenate(parts, axis=0).astype(BF16), spec[q], preferred_element_type=F32)
        acc = part if acc is None else acc + part
    row = 0
    for _, count, stage_ref, out_ref in groups:
        for j in range(2):
            for c in range(lay.cb):
                stage_ref[pl.ds(c * 2 + j, count, stride=lay.per_row), :] = acc[
                    row : row + count, c * LANES : (c + 1) * LANES
                ]
            row += count
        out_ref[...] = stage_ref[...].astype(BF16)


def fetches(lay, spec_ref, buf_ref, sems, begin, n):
    step = lay.slots // PIECES // 16 * 16
    edges = [step * k for k in range(PIECES)] + [lay.slots]
    return [
        [
            pltpu.make_async_copy(
                spec_ref.at[begin + i, q, pl.ds(edges[k], edges[k + 1] - edges[k])],
                buf_ref.at[i, q, pl.ds(edges[k], edges[k + 1] - edges[k])],
                sems.at[i, q, k],
            )
            for q in range(2)
            for k in range(PIECES)
        ]
        for i in range(n)
    ]


def begin_all(copies):
    for group in copies:
        for copy in group:
            copy.start()


def wait_all(copies):
    for copy in copies:
        copy.wait()


def position():
    half = lax.axis_size("lat") // 2
    lat = lax.axis_index("lat")
    return jnp.where(lat < half, 1.0, -1.0).astype(F32), lat % half, lax.axis_index("ma")


def head_kernel(
    pair_hbm, sines_hbm, spec_ref, out_ref, pt_ref, coef_ref, buf_ref, pair_ref, sines_ref, tab_ref, p_ref, stage_ref, small, sems,
    *, lay, n, count, offset,
):
    kept = buf_ref.shape[0]
    copies = fetches(lay, spec_ref, buf_ref, sems, 0, kept)
    pair_copy = pltpu.make_async_copy(pair_hbm, pair_ref, small.at[0])
    sines_copy = pltpu.make_async_copy(sines_hbm, sines_ref, small.at[1])
    pair_copy.start()
    sines_copy.start()
    begin_all(copies)
    sign, band, ma = position()
    pair_copy.wait()
    table_block(lay, pair_ref, tab_ref, coef_ref, 0)
    sines_copy.wait()
    x = gather_rows(lay, sines_ref, band * lay.band, ma * lay.own + offset, count)
    legendre(
        lay, pair_ref, sign, x, coef_ref, p_ref, pt_ref, count,
        lambda block: table_block(lay, pair_ref, tab_ref, coef_ref, block),
    )
    for i in range(kept):
        wait_all(copies[i])
        if i < n:
            project(lay, pair_ref, [(pt_ref, count, stage_ref, out_ref.at[i])], buf_ref.at[i], i)


def kept_kernel(pair_ref, pt_ref, buf_ref, out_ref, stage_ref, *, lay, begin, count):
    for i in range(out_ref.shape[0]):
        project(lay, pair_ref, [(pt_ref, count, stage_ref, out_ref.at[i])], buf_ref.at[begin + i], begin + i)


def late_kernel(*refs, lay, n, begin, count, make):
    refs = list(refs)
    pair_ref = refs.pop(0)
    if make:
        sines_ref, coef_ref = refs.pop(0), refs.pop(0)
    pt_ref = refs.pop(0)
    if lay.split and not make:
        own_pt_ref = refs.pop(0)
    spec_ref, out_ref = refs.pop(0), refs.pop(0)
    if lay.split:
        own_ref = refs.pop(0)
    if make:
        own_pt_ref = refs.pop(0)
    buf_ref, stage_ref, sems = refs.pop(0), refs.pop(0), refs.pop(0)
    copies = fetches(lay, spec_ref, buf_ref, sems, begin, n)
    begin_all(copies)
    if lay.split:
        own_stage_ref = refs.pop(0)
    if make:
        p_ref = refs.pop(0)
        sign, band, ma = position()
        x = gather_rows(lay, sines_ref, band * lay.band, ma * lay.own, lay.own)
        legendre(lay, pair_ref, sign, x, coef_ref, p_ref, own_pt_ref, lay.own, None)
    for i in range(n):
        wait_all(copies[i])
        groups = [(pt_ref, count, stage_ref, out_ref.at[i])]
        if lay.split:
            groups.append((own_pt_ref, lay.own, own_stage_ref, own_ref.at[i]))
        project(lay, pair_ref, groups, buf_ref.at[i], begin + i)


def place_kernel(*refs, plan, sets, peers):
    parts = refs[: len(plan)]
    out_ref, sems = refs[-2], refs[-1]
    ma = lax.axis_index("ma")
    copies = []
    for part, (back, begin) in zip(parts, plan):
        base = lax.rem(ma + (peers - back), peers) * sets + begin
        for i in range(part.shape[0]):
            copies.append(pltpu.make_async_copy(part.at[i], out_ref.at[:, base + i], sems.at[len(copies)]))
    for copy in copies:
        copy.start()
    for copy in copies:
        copy.wait()


def place(parts, plan, shape, sets, peers, out=None):
    count = sum(part.shape[0] for part in parts)
    extra = () if out is None else (out,)
    return pl.pallas_call(
        functools.partial(place_kernel, plan=plan, sets=sets, peers=peers),
        in_specs=[VMEM] * len(parts) + [ANY] * len(extra),
        out_specs=ANY,
        out_shape=jax.ShapeDtypeStruct(shape, BF16),
        scratch_shapes=[pltpu.SemaphoreType.DMA((count,))],
        input_output_aliases={} if out is None else {len(parts): 0},
        compiler_params=PARAMS,
    )(*parts, *extra)


def transform(spectral, set_pair, lat_sines):
    sets, _, slots, cols = spectral.shape
    half = lax.axis_size("lat") // 2
    peers = lax.axis_size("ma")
    band = lat_sines.shape[0] // half
    own = band // peers
    lay = Layout(sets, slots, cols, band, own)
    offset = own if lay.split else 0
    count = band - offset
    cb = lay.cb

    split = lay.split
    pt_shape = jax.ShapeDtypeStruct((lay.high(count) * LANES, lay.padded), F32)
    own_pt_shape = jax.ShapeDtypeStruct((lay.high(own) * LANES, lay.padded), F32)
    coef_shape = jax.ShapeDtypeStruct((3, lay.padded, LANES), F32)

    def p_scratch(rows):
        return pltpu.VMEM((lay.padded * lay.pitch(rows), LANES), F32)

    def out_shape(n, rows):
        return jax.ShapeDtypeStruct((n, rows * lay.per_row, LANES), BF16)

    def stage(rows):
        return pltpu.VMEM((rows * lay.per_row, LANES), F32)

    def keep(value):
        return pltpu.with_memory_space_constraint(value, pltpu.HBM)

    def call(kernel, in_specs, shapes, scratch, args):
        return pl.pallas_call(
            kernel,
            in_specs=in_specs,
            out_specs=[VMEM] * len(shapes),
            out_shape=shapes,
            scratch_shapes=scratch,
            compiler_params=PARAMS,
        )(*args)

    begins = [sum(CHUNKS[:k]) for k in range(len(CHUNKS))]
    kept = sum(CHUNKS[:AHEAD])
    made, mine = [], []
    for k, n in enumerate(CHUNKS):
        if k == 0:
            sent, pt, coef, buf = call(
                functools.partial(head_kernel, lay=lay, n=n, count=count, offset=offset),
                [HBM] * 3,
                [out_shape(n, count), pt_shape, coef_shape, jax.ShapeDtypeStruct((kept, 2, slots, cols), BF16)],
                [
                    pltpu.SMEM(set_pair.shape, jnp.int32),
                    pltpu.SMEM(lat_sines.shape, F32),
                    pltpu.VMEM((3 * lay.rows, lay.padded), F32),
                    p_scratch(count),
                    stage(count),
                    pltpu.SemaphoreType.DMA((2,)),
                    pltpu.SemaphoreType.DMA((kept, 2, PIECES)),
                ],
                [keep(set_pair), keep(lat_sines), keep(spectral)],
            )
        elif k < AHEAD:
            (sent,) = call(
                functools.partial(kept_kernel, lay=lay, begin=begins[k], count=count),
                [SMEM, VMEM, VMEM],
                [out_shape(n, count)],
                [stage(count)],
                [set_pair, pt, buf],
            )
        else:
            make = split and k == AHEAD
            operands = [(SMEM, set_pair)]
            if make:
                operands += [(SMEM, lat_sines), (VMEM, coef)]
            operands.append((VMEM, pt))
            if split and not make:
                operands.append((VMEM, own_pt))
            operands.append((HBM, keep(spectral)))
            shapes = [out_shape(n, count)]
            scratch = [
                pltpu.VMEM((n, 2, slots, cols), BF16),
                stage(count),
                pltpu.SemaphoreType.DMA((n, 2, PIECES)),
            ]
            if split:
                shapes.append(out_shape(n, own))
                scratch.append(stage(own))
            if make:
                shapes.append(own_pt_shape)
                scratch.append(p_scratch(own))
            made_now = call(
                functools.partial(late_kernel, lay=lay, n=n, begin=begins[k], count=count, make=make),
                [spec for spec, _ in operands],
                shapes,
                scratch,
                [value for _, value in operands],
            )
            sent = made_now[0]
            if split:
                mine.append((made_now[1], begins[k]))
            if make:
                own_pt = made_now[2]
        made.append(sent.reshape(n, count // own, own * lay.per_row, LANES))

    first_peer = 0 if split else 1
    early, late = [], []
    for k, (n, parts) in enumerate(zip(CHUNKS, made)):
        if not split:
            mine.append((parts[:, 0], begins[k]))
        for d in range(1, peers):
            moved = lax.ppermute(parts[:, first_peer + d - 1], "ma", [(i, (i + d) % peers) for i in range(peers)])
            (late if k == len(CHUNKS) - 1 else early).append((moved.reshape(n, own, cb, 2, LANES), (d, begins[k])))
    if split:
        (first_own,) = call(
            functools.partial(kept_kernel, lay=lay, begin=0, count=own),
            [SMEM, VMEM, VMEM],
            [out_shape(kept, own)],
            [stage(own)],
            [set_pair, own_pt, buf],
        )
        mine.append((first_own, 0))
    early = [(part.reshape(part.shape[0], own, cb, 2, LANES), (0, begin)) for part, begin in mine] + early
    shape = (own, peers * sets, cb, 2, LANES)
    out = place([p for p, _ in early], [w for _, w in early], shape, sets, peers)
    out = place([p for p, _ in late], [w for _, w in late], shape, sets, peers, out)
    return out.transpose(0, 1, 3, 2, 4).reshape(own, peers * sets, 2, cols)


def solution(mesh):
    placed = (P("ma", None, None, None), P("ma"), P())
    return jax.shard_map(
        transform,
        mesh=mesh,
        in_specs=placed,
        out_specs=P(("lat", "ma"), None, None, None),
        check_vma=False,
    )
```

```python
import functools

import jax
import jax.numpy as jnp
from jax import lax
from jax.experimental import pallas as pl
from jax.experimental.pallas import tpu as pltpu
from jax.sharding import PartitionSpec as P


M = 1280
LANES = 128
F32 = jnp.float32
BF16 = jnp.bfloat16
CHUNKS = (1, 2, 2, 2, 1)
LATE = 2
AHEAD = 2
PIECES = 4
VMEM = pl.BlockSpec(memory_space=pltpu.VMEM)
SMEM = pl.BlockSpec(memory_space=pltpu.SMEM)
ANY = pl.BlockSpec(memory_space=pl.ANY)
HBM = pl.BlockSpec(memory_space=pltpu.HBM)
PARAMS = pltpu.CompilerParams(vmem_limit_bytes=16 << 20)


class Layout:
    def __init__(self, sets, slots, cols, band, own):
        self.sets, self.slots, self.cols, self.band, self.own = sets, slots, cols, band, own
        self.rows = 2 * sets
        self.low = LANES // self.rows
        self.blocks = -(-slots // LANES)
        self.padded = self.blocks * LANES
        self.cb = cols // LANES
        self.split = own % self.low == 0
        self.per_row = 2 * self.cb

    def high(self, count):
        return count // self.low

    def pitch(self, count):
        return -(-self.high(count) // 8) * 8


def coefficients(slot, parity, pair, first_count, count):
    first = slot < first_count
    order = jnp.where(first, pair, M - 1 - pair)
    offset = jnp.where(first, 2 * slot, 2 * (slot - first_count)) + parity
    valid = (offset >= 2) & (slot < count)
    degree = (order + offset).astype(F32)
    square = order.astype(F32) * order.astype(F32)

    def parts(k):
        return k * k - square, 4.0 * k * k - 1.0

    (u0, d0), (u1, d1), (u2, d2), (u3, d3) = (parts(degree - back) for back in range(4))
    u0 = jnp.where(valid, u0, 1.0)
    u1 = jnp.where(valid, u1, 1.0)
    a = jnp.sqrt((d1 / u1) * (d0 / u0))
    b = u1 / d1 + u2 / d2
    g = a * jnp.sqrt(jnp.maximum((u2 / d2) * (u3 / d3), 0.0))
    a, ab, g = (jnp.where(valid, value, 0.0) for value in (a, a * b, g))
    return a, ab, jnp.where(slot == 0, -1.0, g)


def table_block(lay, pair_ref, tab_ref, coef_ref, block):
    rows, sets, low = lay.rows, lay.sets, lay.low
    sub = lax.broadcasted_iota(jnp.int32, (rows, 1), 0)
    pair = jnp.zeros((rows, 1), jnp.int32)
    for s in range(sets):
        pair = jnp.where(sub % sets == s, pair_ref[s], pair)
    parity = sub // sets
    first_count = (M - pair + 1 - parity) // 2
    count = first_count + (pair + 2 - parity) // 2
    here = pl.ds(block * LANES, LANES)
    slot = lax.broadcasted_iota(jnp.int32, (rows, LANES), 1) + block * LANES
    for c, table in enumerate(coefficients(slot, parity, pair, first_count, count)):
        tab_ref[pl.ds(c * rows, rows), here] = table
    for c in range(3):
        wide = [jnp.broadcast_to(tab_ref[pl.ds(c * rows + r, 1), here], (low, LANES)) for r in range(rows)]
        coef_ref[c, here, :] = jnp.concatenate(wide, axis=0).T


def lane_values(lay, pair_ref):
    qs = lax.broadcasted_iota(jnp.int32, (1, LANES), 1) // lay.low
    pair = jnp.zeros((1, LANES), jnp.int32)
    for s in range(lay.sets):
        pair = jnp.where(qs % lay.sets == s, pair_ref[s], pair)
    return pair, qs // lay.sets


def seeds(lay, pair_ref, sign, x):
    sets = lay.sets
    sub = lax.broadcasted_iota(jnp.int32, (sets, 1), 0)
    column = jnp.zeros((sets, 1), jnp.int32)
    for s in range(sets):
        column = jnp.where(sub == s, pair_ref[s], column)
    lane_set = (lax.broadcasted_iota(jnp.int32, (sets, LANES), 1) // lay.low) % sets
    own_set = lane_set == lax.broadcasted_iota(jnp.int32, (sets, LANES), 0)
    pair, parity = lane_values(lay, pair_ref)
    odd = parity > 0
    log_cos = jnp.log(1.0 - x * x)

    def start(order_column, order):
        product = jnp.ones((sets, LANES), F32)
        for block in range(M // LANES):
            k = lax.broadcasted_iota(jnp.int32, (sets, LANES), 1) + (block * LANES + 1)
            product = product * jnp.where(k <= order_column, 1.0 + 0.5 / k.astype(F32), 1.0)
        logs = jnp.sum(jnp.log(product), axis=1, keepdims=True)
        logs = jnp.sum(jnp.where(own_set, logs, 0.0), axis=0, keepdims=True)
        m = order.astype(F32)
        value = jnp.exp(0.5 * (logs + jnp.log(jnp.full((1, LANES), 0.5, F32)) + m * log_cos))
        return jnp.where(odd, sign * jnp.sqrt(2.0 * m + 3.0) * x * value, value)

    first = start(column, pair)
    second = start(M - 1 - column, M - 1 - pair)
    return first, jnp.where(odd & (pair < 1), 0.0, -second)


def gather_rows(lay, sines_ref, begin, first_row, count):
    high = lay.high(count)
    lo = lax.broadcasted_iota(jnp.int32, (high, LANES), 1) % lay.low
    hi = lax.broadcasted_iota(jnp.int32, (high, LANES), 0)
    x = jnp.zeros((high, LANES), F32)
    for h in range(high):
        line = jnp.zeros((1, LANES), F32)
        for l in range(lay.low):
            row = first_row + (h * lay.low + l)
            row = jnp.where(row >= lay.band, row - lay.band, row)
            line = jnp.where(lo[:1] == l, sines_ref[begin + row], line)
        x = jnp.where(hi == h, line, x)
    return x


def legendre(lay, pair_ref, sign, x, coef_ref, p_ref, pt_ref, count, table):
    high, pitch = lay.high(count), lay.pitch(count)
    seed1, seed2 = seeds(lay, pair_ref, sign, x)
    pair, parity = lane_values(lay, pair_ref)
    switch = (M - pair + 1 - parity) // 2
    x2 = x * x
    last, before = jnp.zeros((high, LANES), F32), seed1

    def turn(block, h):
        n = min(LANES, lay.slots - block * LANES)
        tile = p_ref[pl.ds(block * LANES * pitch + h, n, stride=pitch), :]
        pt_ref[pl.ds(h * LANES, LANES), pl.ds(block * LANES, n)] = tile.T

    earliest = (M - (M // 2 - 1)) // 2

    def coef(slot):
        a, b, g = (coef_ref[c, pl.ds(slot, 1), :] for c in range(3))
        return a * x2 - b, g

    def keep(slot, value):
        p_ref[pl.ds(slot * pitch, high), :] = value

    for slot in range(0, lay.slots, 2):
        block, i = divmod(slot, LANES)
        if table is not None and i == LANES // 8 and block + 1 < lay.blocks:
            table(block + 1)
        if block and i >= LANES // 4 and (i - LANES // 4) % 8 == 0 and (i - LANES // 4) // 8 < high:
            turn(block - 1, (i - LANES // 4) // 8)
        (c1, g1), (c2, g2) = coef(slot), coef(slot + 1)
        one = c1 * last - g1 * before
        two = (c2 * c1 - g2) * last
        if slot + 1 >= earliest:
            skip1 = jnp.where(switch == slot, seed2, 0.0)
            one = one - skip1
            two = two - (c2 * skip1 + jnp.where(switch == slot + 1, seed2, 0.0))
        two = two - (c2 * g1) * before
        keep(slot, one)
        keep(slot + 1, two)
        last, before = two, one
    whole = lay.slots // LANES
    for block in range(whole - 1, lay.blocks):
        for h in range(high):
            turn(block, h)


def project(lay, pair_ref, groups, spec, s):
    acc = None
    pair = pair_ref[s]
    here = pl.ds(0, lay.slots)
    for q in range(2):
        base = (q * lay.sets + s) * lay.low
        parts = []
        for pt_ref, count, _, _ in groups:
            w = jnp.concatenate(
                [pt_ref[pl.ds(h * LANES + base, lay.low), here] for h in range(lay.high(count))], axis=0
            )
            first = lax.broadcasted_iota(jnp.int32, (count, lay.slots), 1) < (M - pair + 1 - q) // 2
            parts += [jnp.where(first, w, 0.0), jnp.where(first, 0.0, w)]
        part = jnp.dot(jnp.concatenate(parts, axis=0).astype(BF16), spec[q], preferred_element_type=F32)
        acc = part if acc is None else acc + part
    row = 0
    for _, count, stage_ref, out_ref in groups:
        for j in range(2):
            for c in range(lay.cb):
                stage_ref[pl.ds(c * 2 + j, count, stride=lay.per_row), :] = acc[
                    row : row + count, c * LANES : (c + 1) * LANES
                ]
            row += count
        out_ref[...] = stage_ref[...].astype(BF16)


def fetches(lay, spec_ref, buf_ref, sems, begin, i):
    step = lay.slots // PIECES // 16 * 16
    edges = [step * k for k in range(PIECES)] + [lay.slots]
    return [
        pltpu.make_async_copy(
            spec_ref.at[begin + i, q, pl.ds(edges[k], edges[k + 1] - edges[k])],
            buf_ref.at[i, q, pl.ds(edges[k], edges[k + 1] - edges[k])],
            sems.at[i, q, k],
        )
        for q in range(2)
        for k in range(PIECES)
    ]


def begin_all(lay, spec_ref, buf_ref, sems, begin, n):
    def begin_set(i, carry):
        for copy in fetches(lay, spec_ref, buf_ref, sems, begin, i):
            copy.start()
        return carry

    lax.fori_loop(0, n, begin_set, 0)


def wait_all(copies):
    for copy in copies:
        copy.wait()


def position():
    half = lax.axis_size("lat") // 2
    lat = lax.axis_index("lat")
    return jnp.where(lat < half, 1.0, -1.0).astype(F32), lat % half, lax.axis_index("ma")


def head_kernel(
    pair_hbm, sines_hbm, spec_ref, out_ref, pt_ref, coef_ref, buf_ref, pair_ref, sines_ref, tab_ref, p_ref, stage_ref, small, sems,
    *, lay, n, count, offset,
):
    kept = buf_ref.shape[0]
    pair_copy = pltpu.make_async_copy(pair_hbm, pair_ref, small.at[0])
    sines_copy = pltpu.make_async_copy(sines_hbm, sines_ref, small.at[1])
    pair_copy.start()
    sines_copy.start()
    begin_all(lay, spec_ref, buf_ref, sems, 0, kept)
    sign, band, ma = position()
    pair_copy.wait()
    table_block(lay, pair_ref, tab_ref, coef_ref, 0)
    sines_copy.wait()
    x = gather_rows(lay, sines_ref, band * lay.band, ma * lay.own + offset, count)
    legendre(
        lay, pair_ref, sign, x, coef_ref, p_ref, pt_ref, count,
        lambda block: table_block(lay, pair_ref, tab_ref, coef_ref, block),
    )
    for i in range(kept):
        wait_all(fetches(lay, spec_ref, buf_ref, sems, 0, i))
        if i < n:
            project(lay, pair_ref, [(pt_ref, count, stage_ref, out_ref.at[i])], buf_ref.at[i], i)


def kept_kernel(pair_ref, pt_ref, buf_ref, out_ref, stage_ref, *, lay, begin, count):
    for i in range(out_ref.shape[0]):
        project(lay, pair_ref, [(pt_ref, count, stage_ref, out_ref.at[i])], buf_ref.at[begin + i], begin + i)


def late_kernel(*refs, lay, n, begin, count, make):
    refs = list(refs)
    pair_ref = refs.pop(0)
    if make:
        sines_ref, coef_ref = refs.pop(0), refs.pop(0)
    pt_ref = refs.pop(0)
    if lay.split and not make:
        own_pt_ref = refs.pop(0)
    spec_ref, out_ref = refs.pop(0), refs.pop(0)
    if lay.split:
        own_ref = refs.pop(0)
    if make:
        own_pt_ref = refs.pop(0)
    buf_ref, stage_ref, sems = refs.pop(0), refs.pop(0), refs.pop(0)
    begin_all(lay, spec_ref, buf_ref, sems, begin, n)
    if lay.split:
        own_stage_ref = refs.pop(0)
    if make:
        p_ref = refs.pop(0)
        sign, band, ma = position()
        x = gather_rows(lay, sines_ref, band * lay.band, ma * lay.own, lay.own)
        legendre(lay, pair_ref, sign, x, coef_ref, p_ref, own_pt_ref, lay.own, None)
    for i in range(n):
        wait_all(fetches(lay, spec_ref, buf_ref, sems, begin, i))
        groups = [(pt_ref, count, stage_ref, out_ref.at[i])]
        if lay.split:
            groups.append((own_pt_ref, lay.own, own_stage_ref, own_ref.at[i]))
        project(lay, pair_ref, groups, buf_ref.at[i], begin + i)


def place_kernel(*refs, plan, sets, peers):
    parts = refs[: len(plan)]
    out_ref, sems = refs[-2], refs[-1]
    ma = lax.axis_index("ma")
    copies = []
    for part, (back, begin) in zip(parts, plan):
        base = lax.rem(ma + (peers - back), peers) * sets + begin
        for i in range(part.shape[0]):
            copies.append(pltpu.make_async_copy(part.at[i], out_ref.at[:, base + i], sems.at[len(copies)]))
    for copy in copies:
        copy.start()
    for copy in copies:
        copy.wait()


def place(parts, plan, shape, sets, peers, out=None):
    count = sum(part.shape[0] for part in parts)
    extra = () if out is None else (out,)
    return pl.pallas_call(
        functools.partial(place_kernel, plan=plan, sets=sets, peers=peers),
        in_specs=[VMEM] * len(parts) + [ANY] * len(extra),
        out_specs=ANY,
        out_shape=jax.ShapeDtypeStruct(shape, BF16),
        scratch_shapes=[pltpu.SemaphoreType.DMA((count,))],
        input_output_aliases={} if out is None else {len(parts): 0},
        compiler_params=PARAMS,
    )(*parts, *extra)


def transform(spectral, set_pair, lat_sines):
    sets, _, slots, cols = spectral.shape
    half = lax.axis_size("lat") // 2
    peers = lax.axis_size("ma")
    band = lat_sines.shape[0] // half
    own = band // peers
    lay = Layout(sets, slots, cols, band, own)
    offset = own if lay.split else 0
    count = band - offset
    cb = lay.cb

    split = lay.split
    pt_shape = jax.ShapeDtypeStruct((lay.high(count) * LANES, lay.padded), F32)
    own_pt_shape = jax.ShapeDtypeStruct((lay.high(own) * LANES, lay.padded), F32)
    coef_shape = jax.ShapeDtypeStruct((3, lay.padded, LANES), F32)

    def p_scratch(rows):
        return pltpu.VMEM((lay.padded * lay.pitch(rows), LANES), F32)

    def out_shape(n, rows):
        return jax.ShapeDtypeStruct((n, rows * lay.per_row, LANES), BF16)

    def stage(rows):
        return pltpu.VMEM((rows * lay.per_row, LANES), F32)

    def keep(value):
        return pltpu.with_memory_space_constraint(value, pltpu.HBM)

    def call(kernel, in_specs, shapes, scratch, args):
        return pl.pallas_call(
            kernel,
            in_specs=in_specs,
            out_specs=[VMEM] * len(shapes),
            out_shape=shapes,
            scratch_shapes=scratch,
            compiler_params=PARAMS,
        )(*args)

    begins = [sum(CHUNKS[:k]) for k in range(len(CHUNKS))]
    kept = sum(CHUNKS[:AHEAD])
    made, mine = [], []
    for k, n in enumerate(CHUNKS):
        if k == 0:
            sent, pt, coef, buf = call(
                functools.partial(head_kernel, lay=lay, n=n, count=count, offset=offset),
                [HBM] * 3,
                [out_shape(n, count), pt_shape, coef_shape, jax.ShapeDtypeStruct((kept, 2, slots, cols), BF16)],
                [
                    pltpu.SMEM(set_pair.shape, jnp.int32),
                    pltpu.SMEM(lat_sines.shape, F32),
                    pltpu.VMEM((3 * lay.rows, lay.padded), F32),
                    p_scratch(count),
                    stage(count),
                    pltpu.SemaphoreType.DMA((2,)),
                    pltpu.SemaphoreType.DMA((kept, 2, PIECES)),
                ],
                [keep(set_pair), keep(lat_sines), keep(spectral)],
            )
        elif k < AHEAD:
            (sent,) = call(
                functools.partial(kept_kernel, lay=lay, begin=begins[k], count=count),
                [SMEM, VMEM, VMEM],
                [out_shape(n, count)],
                [stage(count)],
                [set_pair, pt, buf],
            )
        else:
            make = split and k == AHEAD
            operands = [(SMEM, set_pair)]
            if make:
                operands += [(SMEM, lat_sines), (VMEM, coef)]
            operands.append((VMEM, pt))
            if split and not make:
                operands.append((VMEM, own_pt))
            operands.append((HBM, keep(spectral)))
            shapes = [out_shape(n, count)]
            scratch = [
                pltpu.VMEM((n, 2, slots, cols), BF16),
                stage(count),
                pltpu.SemaphoreType.DMA((n, 2, PIECES)),
            ]
            if split:
                shapes.append(out_shape(n, own))
                scratch.append(stage(own))
            if make:
                shapes.append(own_pt_shape)
                scratch.append(p_scratch(own))
            made_now = call(
                functools.partial(late_kernel, lay=lay, n=n, begin=begins[k], count=count, make=make),
                [spec for spec, _ in operands],
                shapes,
                scratch,
                [value for _, value in operands],
            )
            sent = made_now[0]
            if split:
                mine.append((made_now[1], begins[k]))
            if make:
                own_pt = made_now[2]
        made.append(sent.reshape(n, count // own, own * lay.per_row, LANES))

    first_peer = 0 if split else 1
    early, late = [], []
    for k, (n, parts) in enumerate(zip(CHUNKS, made)):
        if not split:
            mine.append((parts[:, 0], begins[k]))
        for d in range(1, peers):
            moved = lax.ppermute(parts[:, first_peer + d - 1], "ma", [(i, (i + d) % peers) for i in range(peers)])
            (late if k >= len(CHUNKS) - LATE else early).append((moved.reshape(n, own, cb, 2, LANES), (d, begins[k])))
    if split:
        (first_own,) = call(
            functools.partial(kept_kernel, lay=lay, begin=0, count=own),
            [SMEM, VMEM, VMEM],
            [out_shape(kept, own)],
            [stage(own)],
            [set_pair, own_pt, buf],
        )
        mine.append((first_own, 0))
    early = [(part.reshape(part.shape[0], own, cb, 2, LANES), (0, begin)) for part, begin in mine] + early
    shape = (own, peers * sets, cb, 2, LANES)
    out = place([p for p, _ in early], [w for _, w in early], shape, sets, peers)
    out = place([p for p, _ in late], [w for _, w in late], shape, sets, peers, out)
    return out.transpose(0, 1, 3, 2, 4).reshape(own, peers * sets, 2, cols)


def solution(mesh):
    placed = (P("ma", None, None, None), P("ma"), P())
    return jax.shard_map(
        transform,
        mesh=mesh,
        in_specs=placed,
        out_specs=P(("lat", "ma"), None, None, None),
        check_vma=False,
    )
```

```python
import functools

import jax
import jax.numpy as jnp
from jax import lax
from jax.experimental import pallas as pl
from jax.experimental.pallas import tpu as pltpu
from jax.sharding import PartitionSpec as P


M = 1280
LANES = 128
F32 = jnp.float32
BF16 = jnp.bfloat16
CHUNKS = (1, 2, 2, 2, 1)
LATE = 2
AHEAD = 2
PIECES = 1
VMEM = pl.BlockSpec(memory_space=pltpu.VMEM)
SMEM = pl.BlockSpec(memory_space=pltpu.SMEM)
ANY = pl.BlockSpec(memory_space=pl.ANY)
HBM = pl.BlockSpec(memory_space=pltpu.HBM)
PARAMS = pltpu.CompilerParams(vmem_limit_bytes=16 << 20)


class Layout:
    def __init__(self, sets, slots, cols, band, own):
        self.sets, self.slots, self.cols, self.band, self.own = sets, slots, cols, band, own
        self.rows = 2 * sets
        self.low = LANES // self.rows
        self.blocks = -(-slots // LANES)
        self.padded = self.blocks * LANES
        self.cb = cols // LANES
        self.split = own % self.low == 0
        self.per_row = 2 * self.cb

    def high(self, count):
        return count // self.low

    def pitch(self, count):
        return -(-self.high(count) // 8) * 8


def coefficients(slot, parity, pair, first_count, count):
    first = slot < first_count
    order = jnp.where(first, pair, M - 1 - pair)
    offset = jnp.where(first, 2 * slot, 2 * (slot - first_count)) + parity
    valid = (offset >= 2) & (slot < count)
    degree = (order + offset).astype(F32)
    square = order.astype(F32) * order.astype(F32)

    def parts(k):
        return k * k - square, 4.0 * k * k - 1.0

    (u0, d0), (u1, d1), (u2, d2), (u3, d3) = (parts(degree - back) for back in range(4))
    u0 = jnp.where(valid, u0, 1.0)
    u1 = jnp.where(valid, u1, 1.0)
    a = jnp.sqrt((d1 / u1) * (d0 / u0))
    b = u1 / d1 + u2 / d2
    g = a * jnp.sqrt(jnp.maximum((u2 / d2) * (u3 / d3), 0.0))
    a, ab, g = (jnp.where(valid, value, 0.0) for value in (a, a * b, g))
    return a, ab, jnp.where(slot == 0, -1.0, g)


def table_block(lay, pair_ref, tab_ref, coef_ref, block):
    rows, sets, low = lay.rows, lay.sets, lay.low
    sub = lax.broadcasted_iota(jnp.int32, (rows, 1), 0)
    pair = jnp.zeros((rows, 1), jnp.int32)
    for s in range(sets):
        pair = jnp.where(sub % sets == s, pair_ref[s], pair)
    parity = sub // sets
    first_count = (M - pair + 1 - parity) // 2
    count = first_count + (pair + 2 - parity) // 2
    here = pl.ds(block * LANES, LANES)
    slot = lax.broadcasted_iota(jnp.int32, (rows, LANES), 1) + block * LANES
    for c, table in enumerate(coefficients(slot, parity, pair, first_count, count)):
        tab_ref[pl.ds(c * rows, rows), here] = table
    for c in range(3):
        wide = [jnp.broadcast_to(tab_ref[pl.ds(c * rows + r, 1), here], (low, LANES)) for r in range(rows)]
        coef_ref[c, here, :] = jnp.concatenate(wide, axis=0).T


def lane_values(lay, pair_ref):
    qs = lax.broadcasted_iota(jnp.int32, (1, LANES), 1) // lay.low
    pair = jnp.zeros((1, LANES), jnp.int32)
    for s in range(lay.sets):
        pair = jnp.where(qs % lay.sets == s, pair_ref[s], pair)
    return pair, qs // lay.sets


def seeds(lay, pair_ref, sign, x):
    sets = lay.sets
    sub = lax.broadcasted_iota(jnp.int32, (sets, 1), 0)
    column = jnp.zeros((sets, 1), jnp.int32)
    for s in range(sets):
        column = jnp.where(sub == s, pair_ref[s], column)
    lane_set = (lax.broadcasted_iota(jnp.int32, (sets, LANES), 1) // lay.low) % sets
    own_set = lane_set == lax.broadcasted_iota(jnp.int32, (sets, LANES), 0)
    pair, parity = lane_values(lay, pair_ref)
    odd = parity > 0
    log_cos = jnp.log(1.0 - x * x)

    def start(order_column, order):
        product = jnp.ones((sets, LANES), F32)
        for block in range(M // LANES):
            k = lax.broadcasted_iota(jnp.int32, (sets, LANES), 1) + (block * LANES + 1)
            product = product * jnp.where(k <= order_column, 1.0 + 0.5 / k.astype(F32), 1.0)
        logs = jnp.sum(jnp.log(product), axis=1, keepdims=True)
        logs = jnp.sum(jnp.where(own_set, logs, 0.0), axis=0, keepdims=True)
        m = order.astype(F32)
        value = jnp.exp(0.5 * (logs + jnp.log(jnp.full((1, LANES), 0.5, F32)) + m * log_cos))
        return jnp.where(odd, sign * jnp.sqrt(2.0 * m + 3.0) * x * value, value)

    first = start(column, pair)
    second = start(M - 1 - column, M - 1 - pair)
    return first, jnp.where(odd & (pair < 1), 0.0, -second)


def gather_rows(lay, sines_ref, begin, first_row, count):
    high = lay.high(count)
    lo = lax.broadcasted_iota(jnp.int32, (high, LANES), 1) % lay.low
    hi = lax.broadcasted_iota(jnp.int32, (high, LANES), 0)
    x = jnp.zeros((high, LANES), F32)
    for h in range(high):
        line = jnp.zeros((1, LANES), F32)
        for l in range(lay.low):
            row = first_row + (h * lay.low + l)
            row = jnp.where(row >= lay.band, row - lay.band, row)
            line = jnp.where(lo[:1] == l, sines_ref[begin + row], line)
        x = jnp.where(hi == h, line, x)
    return x


def legendre(lay, pair_ref, sign, x, coef_ref, p_ref, pt_ref, count, table):
    high, pitch = lay.high(count), lay.pitch(count)
    seed1, seed2 = seeds(lay, pair_ref, sign, x)
    pair, parity = lane_values(lay, pair_ref)
    switch = (M - pair + 1 - parity) // 2
    x2 = x * x
    last, before = jnp.zeros((high, LANES), F32), seed1

    def turn(block, h):
        n = min(LANES, lay.slots - block * LANES)
        tile = p_ref[pl.ds(block * LANES * pitch + h, n, stride=pitch), :]
        tile = tile.astype(BF16).T if n == LANES else tile.T.astype(BF16)
        pt_ref[pl.ds(h * LANES, LANES), pl.ds(block * LANES, n)] = tile

    earliest = (M - (M // 2 - 1)) // 2

    def coef(slot):
        a, b, g = (coef_ref[c, pl.ds(slot, 1), :] for c in range(3))
        return a * x2 - b, g

    def keep(slot, value):
        p_ref[pl.ds(slot * pitch, high), :] = value

    for slot in range(0, lay.slots, 2):
        block, i = divmod(slot, LANES)
        if table is not None and i == LANES // 8:
            for ahead in (1, 2) if block == 0 else (2,):
                if block + ahead < lay.blocks:
                    table(block + ahead)
        if block and i >= LANES // 4 and (i - LANES // 4) % 8 == 0 and (i - LANES // 4) // 8 < high:
            turn(block - 1, (i - LANES // 4) // 8)
        (c1, g1), (c2, g2) = coef(slot), coef(slot + 1)
        one = c1 * last - g1 * before
        two = (c2 * c1 - g2) * last
        if slot + 1 >= earliest:
            skip1 = jnp.where(switch == slot, seed2, 0.0)
            one = one - skip1
            two = two - (c2 * skip1 + jnp.where(switch == slot + 1, seed2, 0.0))
        two = two - (c2 * g1) * before
        keep(slot, one)
        keep(slot + 1, two)
        last, before = two, one
    whole = lay.slots // LANES
    for block in range(whole - 1, lay.blocks):
        for h in range(high):
            turn(block, h)


def project(lay, pairs_ref, groups, spec, s):
    acc = None
    pair = pairs_ref[pl.ds(s, 1), pl.ds(0, lay.slots)]
    here = pl.ds(0, lay.slots)
    for q in range(2):
        base = (q * lay.sets + s) * lay.low
        parts = []
        for pt_ref, count, _, _ in groups:
            pair_base, half = divmod(base, 2 * lay.low)
            w = jnp.concatenate(
                [
                    pt_ref[pl.ds(h * LANES + pair_base * 2 * lay.low, 2 * lay.low), here].astype(F32)[half : half + lay.low]
                    for h in range(lay.high(count))
                ],
                axis=0,
            )
            first = lax.broadcasted_iota(jnp.int32, (count, lay.slots), 1) < lax.shift_right_logical(M - pair + 1 - q, 1)
            parts += [jnp.where(first, w, 0.0), jnp.where(first, 0.0, w)]
        part = jnp.dot(jnp.concatenate(parts, axis=0).astype(BF16), spec[q], preferred_element_type=F32)
        acc = part if acc is None else acc + part
    row = 0
    for _, count, stage_ref, out_ref in groups:
        for j in range(2):
            for c in range(lay.cb):
                stage_ref[pl.ds(c * 2 + j, count, stride=lay.per_row), :] = acc[
                    row : row + count, c * LANES : (c + 1) * LANES
                ]
            row += count
        out_ref[...] = stage_ref[...].astype(BF16)


def fetches(lay, spec_ref, buf_ref, sems, begin, i):
    step = lay.slots // PIECES // 16 * 16
    edges = [step * k for k in range(PIECES)] + [lay.slots]
    return [
        pltpu.make_async_copy(
            spec_ref.at[begin + i, q, pl.ds(edges[k], edges[k + 1] - edges[k])],
            buf_ref.at[i, q, pl.ds(edges[k], edges[k + 1] - edges[k])],
            sems.at[i, q, k],
        )
        for q in range(2)
        for k in range(PIECES)
    ]


def begin_all(lay, spec_ref, buf_ref, sems, begin, n):
    def begin_set(i, carry):
        for copy in fetches(lay, spec_ref, buf_ref, sems, begin, i):
            copy.start()
        return carry

    lax.fori_loop(0, n, begin_set, 0)


def wait_all(copies):
    for copy in copies:
        copy.wait()


def position():
    half = lax.axis_size("lat") // 2
    lat = lax.axis_index("lat")
    return jnp.where(lat < half, 1.0, -1.0).astype(F32), lat % half, lax.axis_index("ma")


def head_kernel(
    pair_hbm, sines_hbm, spec_ref, out_ref, pt_ref, coef_ref, buf_ref, pairs_ref, pair_ref, sines_ref, tab_ref, p_ref, stage_ref, small, sems,
    *, lay, n, count, offset,
):
    kept = buf_ref.shape[0]
    pair_copy = pltpu.make_async_copy(pair_hbm, pair_ref, small.at[0])
    sines_copy = pltpu.make_async_copy(sines_hbm, sines_ref, small.at[1])
    pair_copy.start()
    sines_copy.start()
    begin_all(lay, spec_ref, buf_ref, sems, 0, kept)
    sign, band, ma = position()
    pair_copy.wait()
    sines_copy.wait()
    for s in range(lay.sets):
        pairs_ref[pl.ds(s, 1), :] = jnp.full((1, lay.padded), pair_ref[s], jnp.int32)
    table_block(lay, pair_ref, tab_ref, coef_ref, 0)
    x = gather_rows(lay, sines_ref, band * lay.band, ma * lay.own + offset, count)
    legendre(
        lay, pair_ref, sign, x, coef_ref, p_ref, pt_ref, count,
        lambda block: table_block(lay, pair_ref, tab_ref, coef_ref, block),
    )
    for i in range(kept):
        wait_all(fetches(lay, spec_ref, buf_ref, sems, 0, i))
        if i < n:
            project(lay, pairs_ref, [(pt_ref, count, stage_ref, out_ref.at[i])], buf_ref.at[i], i)


def kept_kernel(pairs_ref, pt_ref, buf_ref, out_ref, stage_ref, *, lay, begin, count):
    for i in range(out_ref.shape[0]):
        project(lay, pairs_ref, [(pt_ref, count, stage_ref, out_ref.at[i])], buf_ref.at[begin + i], begin + i)


def late_kernel(*refs, lay, n, begin, count, make):
    refs = list(refs)
    pairs_ref = refs.pop(0)
    if make:
        pair_ref, sines_ref, coef_ref = refs.pop(0), refs.pop(0), refs.pop(0)
    pt_ref = refs.pop(0)
    if lay.split and not make:
        own_pt_ref = refs.pop(0)
    spec_ref, out_ref = refs.pop(0), refs.pop(0)
    if lay.split:
        own_ref = refs.pop(0)
    if make:
        own_pt_ref = refs.pop(0)
    buf_ref, stage_ref, sems = refs.pop(0), refs.pop(0), refs.pop(0)
    begin_all(lay, spec_ref, buf_ref, sems, begin, n)
    if lay.split:
        own_stage_ref = refs.pop(0)
    if make:
        p_ref = refs.pop(0)
        sign, band, ma = position()
        x = gather_rows(lay, sines_ref, band * lay.band, ma * lay.own, lay.own)
        legendre(lay, pair_ref, sign, x, coef_ref, p_ref, own_pt_ref, lay.own, None)
    for i in range(n):
        wait_all(fetches(lay, spec_ref, buf_ref, sems, begin, i))
        groups = [(pt_ref, count, stage_ref, out_ref.at[i])]
        if lay.split:
            groups.append((own_pt_ref, lay.own, own_stage_ref, own_ref.at[i]))
        project(lay, pairs_ref, groups, buf_ref.at[i], begin + i)


def place_kernel(*refs, plan, sets, peers):
    parts = refs[: len(plan)]
    out_ref, sems = refs[-2], refs[-1]
    ma = lax.axis_index("ma")
    copies = []
    for part, (back, begin) in zip(parts, plan):
        base = lax.rem(ma + (peers - back), peers) * sets + begin
        for i in range(part.shape[0]):
            copies.append(pltpu.make_async_copy(part.at[i], out_ref.at[:, base + i], sems.at[len(copies)]))
    for copy in copies:
        copy.start()
    for copy in copies:
        copy.wait()


def place(parts, plan, shape, sets, peers, out=None):
    count = sum(part.shape[0] for part in parts)
    extra = () if out is None else (out,)
    return pl.pallas_call(
        functools.partial(place_kernel, plan=plan, sets=sets, peers=peers),
        in_specs=[VMEM] * len(parts) + [ANY] * len(extra),
        out_specs=ANY,
        out_shape=jax.ShapeDtypeStruct(shape, BF16),
        scratch_shapes=[pltpu.SemaphoreType.DMA((count,))],
        input_output_aliases={} if out is None else {len(parts): 0},
        compiler_params=PARAMS,
    )(*parts, *extra)


def transform(spectral, set_pair, lat_sines):
    sets, _, slots, cols = spectral.shape
    half = lax.axis_size("lat") // 2
    peers = lax.axis_size("ma")
    band = lat_sines.shape[0] // half
    own = band // peers
    lay = Layout(sets, slots, cols, band, own)
    offset = own if lay.split else 0
    count = band - offset
    cb = lay.cb

    split = lay.split
    pt_shape = jax.ShapeDtypeStruct((lay.high(count) * LANES, lay.padded), BF16)
    own_pt_shape = jax.ShapeDtypeStruct((lay.high(own) * LANES, lay.padded), BF16)
    coef_shape = jax.ShapeDtypeStruct((3, lay.padded, LANES), F32)

    pairs_shape = jax.ShapeDtypeStruct((sets, lay.padded), jnp.int32)

    def p_scratch(rows):
        return pltpu.VMEM((lay.padded * lay.pitch(rows), LANES), F32)

    def out_shape(n, rows):
        return jax.ShapeDtypeStruct((n, rows * lay.per_row, LANES), BF16)

    def stage(rows):
        return pltpu.VMEM((rows * lay.per_row, LANES), F32)

    def keep(value):
        return pltpu.with_memory_space_constraint(value, pltpu.HBM)

    def call(kernel, in_specs, shapes, scratch, args):
        return pl.pallas_call(
            kernel,
            in_specs=in_specs,
            out_specs=[VMEM] * len(shapes),
            out_shape=shapes,
            scratch_shapes=scratch,
            compiler_params=PARAMS,
        )(*args)

    begins = [sum(CHUNKS[:k]) for k in range(len(CHUNKS))]
    kept = sum(CHUNKS[:AHEAD])
    made, mine = [], []
    for k, n in enumerate(CHUNKS):
        if k == 0:
            sent, pt, coef, buf, pairs = call(
                functools.partial(head_kernel, lay=lay, n=n, count=count, offset=offset),
                [HBM] * 3,
                [out_shape(n, count), pt_shape, coef_shape, jax.ShapeDtypeStruct((kept, 2, slots, cols), BF16), pairs_shape],
                [
                    pltpu.SMEM(set_pair.shape, jnp.int32),
                    pltpu.SMEM(lat_sines.shape, F32),
                    pltpu.VMEM((3 * lay.rows, lay.padded), F32),
                    p_scratch(count),
                    stage(count),
                    pltpu.SemaphoreType.DMA((2,)),
                    pltpu.SemaphoreType.DMA((kept, 2, PIECES)),
                ],
                [keep(set_pair), keep(lat_sines), keep(spectral)],
            )
        elif k < AHEAD:
            (sent,) = call(
                functools.partial(kept_kernel, lay=lay, begin=begins[k], count=count),
                [VMEM, VMEM, VMEM],
                [out_shape(n, count)],
                [stage(count)],
                [pairs, pt, buf],
            )
        else:
            make = split and k == AHEAD
            operands = [(VMEM, pairs)]
            if make:
                operands += [(SMEM, set_pair), (SMEM, lat_sines), (VMEM, coef)]
            operands.append((VMEM, pt))
            if split and not make:
                operands.append((VMEM, own_pt))
            operands.append((HBM, keep(spectral)))
            shapes = [out_shape(n, count)]
            scratch = [
                pltpu.VMEM((n, 2, slots, cols), BF16),
                stage(count),
                pltpu.SemaphoreType.DMA((n, 2, PIECES)),
            ]
            if split:
                shapes.append(out_shape(n, own))
                scratch.append(stage(own))
            if make:
                shapes.append(own_pt_shape)
                scratch.append(p_scratch(own))
            made_now = call(
                functools.partial(late_kernel, lay=lay, n=n, begin=begins[k], count=count, make=make),
                [spec for spec, _ in operands],
                shapes,
                scratch,
                [value for _, value in operands],
            )
            sent = made_now[0]
            if split:
                mine.append((made_now[1], begins[k]))
            if make:
                own_pt = made_now[2]
        made.append(sent.reshape(n, count // own, own * lay.per_row, LANES))

    first_peer = 0 if split else 1
    early, late = [], [[] for _ in range(LATE)]
    for k, (n, parts) in enumerate(zip(CHUNKS, made)):
        if not split:
            mine.append((parts[:, 0], begins[k]))
        for d in range(1, peers):
            moved = lax.ppermute(parts[:, first_peer + d - 1], "ma", [(i, (i + d) % peers) for i in range(peers)])
            group = early if k < len(CHUNKS) - LATE else late[k - len(CHUNKS)]
            group.append((moved.reshape(n, own, cb, 2, LANES), (d, begins[k])))
    if split:
        (first_own,) = call(
            functools.partial(kept_kernel, lay=lay, begin=0, count=own),
            [VMEM, VMEM, VMEM],
            [out_shape(kept, own)],
            [stage(own)],
            [pairs, own_pt, buf],
        )
        mine.append((first_own, 0))
    early = [(part.reshape(part.shape[0], own, cb, 2, LANES), (0, begin)) for part, begin in mine] + early
    shape = (own, peers * sets, cb, 2, LANES)
    out = place([p for p, _ in early], [w for _, w in early], shape, sets, peers)
    for group in late:
        out = place([p for p, _ in group], [w for _, w in group], shape, sets, peers, out)
    return out.transpose(0, 1, 3, 2, 4).reshape(own, peers * sets, 2, cols)


def solution(mesh):
    placed = (P("ma", None, None, None), P("ma"), P())
    return jax.shard_map(
        transform,
        mesh=mesh,
        in_specs=placed,
        out_specs=P(("lat", "ma"), None, None, None),
        check_vma=False,
    )
```
